128 devices in a mesh: ctx: 32 (over x, y, core), tp: 4 (over z).
Axes of the slice: x: 4, y: 4, z: 4, core: 2. Of those that a mesh axis runs over, the one named last changes fastest.
Arguments:
- tokens: bfloat16 [32768, 2048], P('ctx'), may hold values from -6 to 6
- w_value: bfloat16 [2048, 4096], P(None, 'tp'), may hold values from -0.125 to 0.125
- w_gate: bfloat16 [2048, 4096], P(None, 'tp'), may hold values from -0.125 to 0.125
- w_state: bfloat16 [2048, 256], replicated, may hold values from -0.125 to 0.125
- w_level: bfloat16 [2048, 512], P(None, 'tp'), may hold values from -0.125 to 0.125
- log_decay: float32 [32768, 64], P('ctx', 'tp'), may hold values from -1.6 to 0
- skip_weight: float32 [64], P('tp'), may hold values from 0.5 to 1.5
- norm_gain: float32 [4096], P('tp'), may hold values from 0.5 to 1.5
- doc_ids: int32 [128], replicated, may hold values from 0 to 3, as said below
- w_out: bfloat16 [4096, 2048], P('tp'), may hold values from -0.09375 to 0.09375
Outputs:
- mixed: bfloat16 [32768, 2048], P('ctx', 'tp')
The draws below stay inside these ranges and needn't reach their ends.
Inputs may be any that keep to these rules, and one draw needn't show every extreme that they name: `doc_ids`: is non-decreasing along the stretches; each document is a run of whole stretches; all 4 documents occur; the longest holds exactly 65 stretches.
All inputs are finite; a program needn't handle non-finite values.
Results may differ from the reference program's by a relative error of at most 0.022.
Values may be sent and summed in bfloat16 or wider, within the bound.
No kernel may reach another device: no remote copies, remote signals or barrier semaphores. Data moves between devices by JAX's collectives and lax.ppermute only.
A program may use at most 128 MiB of HBM per device.

```python
import jax
import jax.numpy as jnp
from jax import lax

D = 2048
HEAD_TOTAL = 64
P_SIZE = 64
N = 128
STRETCH = 256
STRETCHES_DEV = 4
NC = 128
TOKENS = 32768
DI = 4096
LEVELS = 8
N_TP = 4


def draw_log_decay(key, part):
    random_child_keys = jax.random.split(key, 8)
    long_share = 0.4
    middle_share = 0.45
    head_class = jax.random.uniform(random_child_keys[0], (HEAD_TOTAL,))
    is_long = head_class < long_share
    is_middle = (head_class >= long_share) & (head_class < long_share + middle_share)
    slow_rate = jnp.exp(jax.random.uniform(random_child_keys[1], (HEAD_TOTAL,), minval=jnp.log(0.03 / TOKENS), maxval=jnp.log(0.3 / TOKENS)))
    fast_rate = jnp.exp(jax.random.uniform(random_child_keys[2], (HEAD_TOTAL,), minval=jnp.log(1.0 / 500.0), maxval=jnp.log(1.0 / 30.0)))
    middle_total = jnp.exp(jax.random.uniform(random_child_keys[7], (HEAD_TOTAL,), minval=jnp.log(0.06), maxval=jnp.log(0.2)))
    middle_rate = middle_total / (1.25 * STRETCH)
    decay_rate = jnp.where(is_long, slow_rate, jnp.where(is_middle, middle_rate, fast_rate))
    token_factor = jax.random.uniform(random_child_keys[3], (TOKENS, HEAD_TOTAL), minval=0.5, maxval=2.0)
    block_factor = jnp.repeat(jax.random.uniform(random_child_keys[4], (NC, HEAD_TOTAL), minval=0.5, maxval=2.0), STRETCH, axis=0)
    decay_amounts = -decay_rate[None, :] * token_factor * block_factor
    location_lookup = jax.random.randint(random_child_keys[5], (2, HEAD_TOTAL), 0, TOKENS)
    spike_penalty = jax.random.uniform(random_child_keys[6], (2, HEAD_TOTAL), minval=0.2, maxval=0.5)
    head_position = jnp.broadcast_to(jnp.arange(HEAD_TOTAL), (2, HEAD_TOTAL))
    decay_amounts = decay_amounts.at[location_lookup, head_position].add(jnp.log1p(-spike_penalty))
    return decay_amounts.astype(jnp.float32)


def draw_doc_ids(key, part):
    child_keys = jax.random.split(key, 3)
    long_len = NC // 2 + 1
    first = jax.random.randint(child_keys[0], (), 0, STRETCHES_DEV)
    rest_start = first + long_len
    first_cut = jax.random.randint(child_keys[1], (), rest_start + 1, NC - 1)
    second_cut = jax.random.randint(child_keys[2], (), first_cut + 1, NC)
    positions = jnp.arange(NC, dtype=jnp.int32)
    starts_at_zero = (first == 0).astype(jnp.int32)
    labels = (positions >= first).astype(jnp.int32) + (positions >= rest_start).astype(jnp.int32) + (positions >= first_cut).astype(jnp.int32) + starts_at_zero * (positions >= second_cut).astype(jnp.int32) - starts_at_zero
    return labels.astype(jnp.int32)


def shard_levels(own_key, extent, cuts, smallest, largest):
    level, own = 1.0, jax.random.fold_in(own_key, 6)
    for axis_at, shards_of in cuts:
        draws = jnp.exp(jax.random.uniform(jax.random.fold_in(own, axis_at), (shards_of,), jnp.float32, smallest / len(cuts), largest / len(cuts)))
        level = level * jnp.repeat(draws, extent[axis_at] // shards_of).reshape([-1 if axis == axis_at else 1 for axis in range(len(extent))])
    return level


def noise(key, dims, spread, reach, pieces=(), kind=jnp.bfloat16):
    loudness = shard_levels(key, dims, pieces, -0.22, 0.18) if pieces else 1.0
    values = jax.random.normal(key, dims, jnp.float32) * spread * loudness
    return jnp.minimum(jnp.maximum(values, -reach), reach).astype(kind)


def setup_inputs(seed: int = 0) -> dict:
    key_of = jax.random.split(jax.random.key(seed), 11)
    return {
        "tokens": noise(key_of[0], (TOKENS, D), 1.0, 6.0, ((0, 32),)),
        "w_value": noise(key_of[1], (D, DI), D ** -0.5, 0.125, ((1, 4),)),
        "w_gate": noise(key_of[2], (D, DI), D ** -0.5, 0.125, ((1, 4),)),
        "w_state": noise(key_of[3], (D, 2 * N), D ** -0.5, 0.125),
        "w_level": noise(key_of[4], (D, HEAD_TOTAL * LEVELS), D ** -0.5, 0.125, ((1, 4),)),
        "log_decay": draw_log_decay(jax.random.fold_in(key_of[10], 71), 0),
        "skip_weight": jnp.clip(0.5 + 1.0 * jax.random.uniform(key_of[6], (HEAD_TOTAL,), jnp.float32) ** shard_levels(key_of[6], (HEAD_TOTAL,), ((0, 4),), -0.2, 0.2), 0.5, 1.5),
        "norm_gain": jnp.clip(0.5 + 1.0 * jax.random.uniform(key_of[7], (DI,), jnp.float32) ** shard_levels(key_of[7], (DI,), ((0, 4),), -0.2, 0.2), 0.5, 1.5),
        "doc_ids": draw_doc_ids(jax.random.fold_in(key_of[10], 71), 0),
        "w_out": noise(key_of[9], (DI, D), DI ** -0.5, 0.09375, ((0, 4),)),
    }


def rounded(operand):
    return lax.optimization_barrier(operand.astype(jnp.bfloat16)).astype(jnp.float32)

def bit_length_of(operand):
    length_sum = jnp.zeros_like(operand)
    for shift_by in range(31):
        length_sum = length_sum + (operand >> shift_by > 0).astype(jnp.int32)
    return length_sum

def reference(tokens, w_value, w_gate, w_state, w_level, log_decay, skip_weight, norm_gain, doc_ids, w_out):
    stretches = tokens.reshape(NC, STRETCH, D)
    decays = log_decay.reshape(NC, STRETCH, HEAD_TOTAL)
    causal = jnp.tril(jnp.ones((STRETCH, STRETCH), bool))
    level_ids = jnp.arange(LEVELS - 1, dtype=jnp.int32)
    group_cols = HEAD_TOTAL * P_SIZE // N_TP
    highest = lax.Precision.HIGHEST

    def advance(running, stretch_index):
        levels, prev_doc = running
        stretch_rows = lax.dynamic_index_in_dim(stretches, stretch_index, keepdims=False)
        decays_now = lax.dynamic_index_in_dim(decays, stretch_index, keepdims=False)
        doc_now = lax.dynamic_index_in_dim(doc_ids, stretch_index, keepdims=False)
        levels = jnp.where(doc_now == prev_doc, levels, jnp.zeros_like(levels))
        head_vals = rounded(jnp.dot(stretch_rows, w_value, preferred_element_type=jnp.float32)).reshape(STRETCH, HEAD_TOTAL, P_SIZE)
        gates = rounded(jnp.dot(stretch_rows, w_gate, preferred_element_type=jnp.float32))
        state_proj = jnp.dot(stretch_rows, w_state, preferred_element_type=jnp.float32).astype(jnp.bfloat16)
        b_input = state_proj[:, :N]
        c_output = state_proj[:, N:]
        level_mixing_weight = jax.nn.softplus(rounded(jnp.dot(stretch_rows, w_level, preferred_element_type=jnp.float32))).reshape(STRETCH, HEAD_TOTAL, LEVELS)
        decay_cum = jnp.cumsum(decays_now, axis=0)
        stretch_total = decay_cum[-1]
        scores = jnp.dot(c_output, b_input.T, preferred_element_type=jnp.float32)
        decay_gap = decay_cum[:, None, :] - decay_cum[None, :, :]
        decay_mask = jnp.exp(jnp.where(causal[:, :, None], decay_gap, -1e+30))
        weights = rounded(scores[:, :, None] * decay_mask)
        intra_term = jnp.einsum('tsh,shp->thp', weights, head_vals, precision=highest)
        weighted_b = rounded(jnp.exp(stretch_total[None, :] - decay_cum)[:, :, None] * b_input.astype(jnp.float32)[:, None, :])
        stretch_state = jnp.einsum('shn,shp->hnp', weighted_b, head_vals, precision=highest)
        level_bf = rounded(levels)
        level_grid = jnp.einsum('tn,lhnp->thlp', c_output.astype(jnp.float32), level_bf, precision=highest)
        cross_term = lax.optimization_barrier(jnp.sum(level_mixing_weight[:, :, 1:, None] * level_grid, axis=2)) * jnp.exp(decay_cum)[:, :, None]
        head_out = skip_weight[None, :, None] * head_vals + level_mixing_weight[:, :, :1] * intra_term + cross_term
        gated = head_out * jax.nn.silu(gates).reshape(STRETCH, HEAD_TOTAL, P_SIZE)
        inv_rms = lax.rsqrt(lax.optimization_barrier(jnp.mean(gated * gated, axis=2, keepdims=True)) + 1e-05)
        normed = ((gated * inv_rms).reshape(STRETCH, HEAD_TOTAL * P_SIZE) * norm_gain[None, :]).astype(jnp.bfloat16)
        out_rows = jnp.zeros((STRETCH, D), jnp.float32)
        for group_index in range(N_TP):
            lower_col = group_index * group_cols
            partial_value = jnp.dot(normed[:, lower_col:lower_col + group_cols], w_out[lower_col:lower_col + group_cols], preferred_element_type=jnp.float32)
            out_rows = out_rows + rounded(partial_value)
        following = stretch_index + 1
        lowest = following & -following
        merge_level = bit_length_of(lowest) - 1
        factor = jnp.exp(stretch_total)[None, :, None, None]
        kept_levels = jnp.where((level_ids > merge_level)[:, None, None, None], levels * factor, 0.0)
        merged = lax.optimization_barrier(jnp.sum(jnp.where((level_ids <= merge_level)[:, None, None, None], levels, 0.0), axis=0)) * factor[0] + stretch_state
        new_levels = kept_levels + jnp.where((level_ids == merge_level)[:, None, None, None], merged[None], 0.0)
        return ((new_levels, doc_now), out_rows.astype(jnp.bfloat16))
    start_levels = jnp.zeros((LEVELS - 1, HEAD_TOTAL, N, P_SIZE), jnp.float32)
    indices = jnp.arange(NC, dtype=jnp.int32)
    final, outputs = lax.scan(advance, (start_levels, doc_ids[0]), indices)
    return outputs.reshape(TOKENS, D)
```

```python
import functools

import jax
import jax.numpy as jnp
from jax import lax
from jax.experimental import pallas as pl
from jax.experimental.pallas import tpu as pltpu
from jax.sharding import PartitionSpec as P

STRETCH = 256
HEAD = 64
STATE = 128
LEVELS = 8
F32 = jnp.float32
BF16 = jnp.bfloat16
HIGHEST = lax.Precision.HIGHEST
NT = (((1,), (1,)), ((), ()))
CHUNKS = ((0, 1), (1, 2), (2, 3), (3, 4))
VMEM_BYTES = 56 << 20


def dot(a, b):
    return jnp.dot(a, b, preferred_element_type=F32)


def dot_nt(a, b):
    return lax.dot_general(a, b, NT, preferred_element_type=F32)


def iota(shape, dim):
    return lax.broadcasted_iota(jnp.int32, shape, dim)


def decay_rows(log_decay):
    tokens, heads = log_decay.shape
    eye = (iota((heads, heads), 0) == iota((heads, heads), 1)).astype(F32)
    turned = lax.dot_general(eye, log_decay, NT, precision=HIGHEST, preferred_element_type=F32)
    upper = (iota((tokens, tokens), 0) <= iota((tokens, tokens), 1)).astype(F32)
    cum = jnp.dot(turned, upper, precision=HIGHEST, preferred_element_type=F32)
    total = jnp.broadcast_to(cum[:, tokens - 1 : tokens], (heads, STATE))
    return cum, total


def project_kernel(
    meta, docs, tok, w_value, w_state, log_decay, v_out, sp_out, local_out, pay_out, run, scaled, run_total
):
    step = pl.program_id(0)
    heads = log_decay.shape[1]
    tokens = tok[...]
    state_proj = dot(tokens, w_state[...]).astype(BF16)
    sp_out[...] = state_proj
    cum, total = decay_rows(log_decay[...])
    v_out[0] = jnp.transpose(dot(tokens, w_value[...]).astype(BF16))
    tail = jnp.exp(jnp.concatenate([total, total], axis=1) - cum)
    for h in range(heads):
        rows = pl.ds(h * HEAD, HEAD)
        scaled[rows, :] = (v_out[0, rows, :].astype(F32) * tail[h : h + 1, :]).astype(BF16)
    state = dot(scaled[...], state_proj[:, :STATE])
    first = meta[0] * pl.num_programs(0)

    @pl.when(step == 0)
    def _():
        run[...] = jnp.zeros_like(run)
        run_total[...] = jnp.zeros_like(run_total)

    before = docs[first + jnp.maximum(step - 1, 0)]
    same = (before == docs[first + step]).astype(F32)
    factor = jnp.exp(total) * same
    for h in range(heads):
        rows = pl.ds(h * HEAD, HEAD)
        run[rows, :] = run[rows, :] * factor[h : h + 1, :] + state[h * HEAD : (h + 1) * HEAD, :]
    run_total[...] = run_total[...] + total

    @pl.when(step == 0)
    def _():
        local_out[0] = state.astype(BF16)

    @pl.when(step == 1)
    def _():
        local_out[1] = run[...].astype(BF16)

    @pl.when(step == 2)
    def _():
        local_out[2] = state.astype(BF16)

    @pl.when(step == 3)
    def _():
        top = heads * HEAD
        pay_out[pl.ds(0, top), :] = run[...].astype(BF16)
        store_total(pay_out, top, run_total[...])


def store_total(ref, top, total):
    heads = total.shape[0]
    high = total.astype(BF16)
    rest = total - high.astype(F32)
    middle = rest.astype(BF16)
    low = (rest - middle.astype(F32)).astype(BF16)
    ref[pl.ds(top, heads), :] = high
    ref[pl.ds(top + heads, heads), :] = middle
    ref[pl.ds(top + 2 * heads, heads), :] = low


def load_total(ref, top, heads):
    parts = [ref[pl.ds(top + k * heads, heads), :].astype(F32) for k in range(3)]
    return (parts[0] + parts[1]) + parts[2]


def project(meta, docs, tokens, w_value, w_state, log_decay):
    rows, depth = tokens.shape
    heads = log_decay.shape[1]
    width = w_value.shape[1]
    steps = rows // STRETCH
    smem = pl.BlockSpec(memory_space=pltpu.SMEM)
    one = pl.Buffered(1)
    return pl.pallas_call(
        project_kernel,
        name="project",
        grid=(steps,),
        in_specs=[
            smem,
            smem,
            pl.BlockSpec((STRETCH, depth), lambda i: (i, 0)),
            pl.BlockSpec((depth, width), lambda i: (0, 0), pipeline_mode=one),
            pl.BlockSpec((depth, 2 * STATE), lambda i: (0, 0), pipeline_mode=one),
            pl.BlockSpec((STRETCH, heads), lambda i: (i, 0)),
        ],
        out_specs=[
            pl.BlockSpec((1, width, STRETCH), lambda i: (i, 0, 0)),
            pl.BlockSpec((STRETCH, 2 * STATE), lambda i: (i, 0)),
            pl.BlockSpec((3, width, STATE), lambda i: (0, 0, 0)),
            pl.BlockSpec((width + 3 * heads, STATE), lambda i: (0, 0)),
        ],
        out_shape=[
            jax.ShapeDtypeStruct((steps, width, STRETCH), BF16),
            jax.ShapeDtypeStruct((rows, 2 * STATE), BF16),
            jax.ShapeDtypeStruct((3, width, STATE), BF16),
            jax.ShapeDtypeStruct((width + 3 * heads, STATE), BF16),
        ],
        scratch_shapes=[
            pltpu.VMEM((width, STATE), F32),
            pltpu.VMEM((width, STRETCH), BF16),
            pltpu.VMEM((heads, STATE), F32),
        ],
        compiler_params=pltpu.CompilerParams(vmem_limit_bytes=VMEM_BYTES),
        cost_estimate=pl.CostEstimate(
            flops=2 * rows * depth * (width + 2 * STATE),
            bytes_accessed=2 * (rows * depth + depth * width + rows * width),
            transcendentals=0,
        ),
    )(meta, docs, tokens, w_value, w_state, log_decay)


def combine_kernel(bit, heads_here, offset_by_core, meta, docs, own, peer, earlier, pay_out, earlier_out):
    heads = earlier.shape[0]
    ctx = meta[0]
    per_dev = docs.shape[0] // (1 << 5)
    base = (ctx >> (bit + 1)) << (bit + 1)
    last_left = docs[(base + (1 << bit)) * per_dev - 1]
    last_right = docs[(base + (2 << bit)) * per_dev - 1]
    same = (last_left == last_right).astype(F32)
    is_right = ((ctx >> bit) & 1) == 1
    core = ctx & 1
    own_top = own.shape[0] - 3 * heads
    total_own = load_total(own, own_top, heads)
    total_peer = load_total(peer, own_top, heads)
    factor = jnp.exp(jnp.where(is_right, total_own, total_peer)) * same
    own_by = jnp.where(is_right, 1.0, factor)
    peer_by = jnp.where(is_right, factor, 1.0)
    for half in range(2):

        @pl.when(core == half)
        def _(half=half):
            for h in range(heads_here):
                g = h + half * heads_here
                at = pl.ds((g if offset_by_core else h) * HEAD, HEAD)
                pay_out[pl.ds(h * HEAD, HEAD), :] = (
                    own[at, :].astype(F32) * own_by[g : g + 1, :] + peer[at, :].astype(F32) * peer_by[g : g + 1, :]
                ).astype(BF16)

    store_total(pay_out, heads_here * HEAD, total_own + total_peer)
    earlier_out[...] = earlier[...] + jnp.where(is_right, total_peer, 0.0)


def combine(bit, meta, docs, own, peer, earlier, half):
    heads = earlier.shape[0]
    here = heads // 2
    smem = pl.BlockSpec(memory_space=pltpu.SMEM)
    vmem = pl.BlockSpec(memory_space=pltpu.VMEM)
    return pl.pallas_call(
        functools.partial(combine_kernel, bit, here, not half),
        name=f"combine{bit}",
        in_specs=[smem, smem, vmem, vmem, vmem],
        out_specs=[vmem, vmem],
        out_shape=[
            jax.ShapeDtypeStruct((here * HEAD + 3 * heads, STATE), BF16),
            jax.ShapeDtypeStruct((heads, STATE), F32),
        ],
        cost_estimate=pl.CostEstimate(flops=1 << 20, bytes_accessed=1 << 20, transcendentals=0),
    )(meta, docs, own, peer, earlier)


def intra_kernel(
    index, meta, docs, skip, tok, w_gate, w_level, v, sp, log_decay, local, start, gate_out, ho_out, lw_out, start_out
):
    heads = log_decay.shape[1]
    tokens = tok[...]
    gate_out[...] = jnp.transpose(dot(tokens, w_gate[...]).astype(BF16))
    level_pre = dot(tokens, w_level[...]).astype(BF16)
    cols = heads * LEVELS
    to_row, from_col = iota((cols, cols), 0), iota((cols, cols), 1)
    pick = ((to_row % heads) * LEVELS + to_row // heads == from_col).astype(BF16)
    turned = dot_nt(pick, level_pre)
    weight = jnp.maximum(turned, 0.0) + jnp.log1p(jnp.exp(-jnp.abs(turned)))
    cum, total = decay_rows(log_decay[...])
    lower = (iota((STRETCH, STRETCH), 0) >= iota((STRETCH, STRETCH), 1)).astype(F32)
    cum_col = jnp.dot(lower, log_decay[...], precision=HIGHEST, preferred_element_type=F32)
    begin = start[pl.ds(0, heads), :]
    previous = start[pl.ds(heads, heads), :]
    start_out[pl.ds(0, heads), :] = begin + total
    start_out[pl.ds(heads, heads), :] = total
    grown = jnp.exp(cum)
    from_device = jnp.exp(cum + jnp.concatenate([begin, begin], axis=1))
    for level in range(LEVELS):
        rows = slice(level * heads, (level + 1) * heads)
        lw_out[pl.ds(level * heads, heads), :] = weight[rows] * from_device
    b_in = sp[:, :STATE]
    c_out = sp[:, STATE:]
    scores = dot_nt(b_in, c_out)
    causal = iota((128, 128), 0) <= iota((128, 128), 1)
    first = meta[0] * 4
    terms = []
    if index & 1:
        keep = (docs[first + index - 1] == docs[first + index]).astype(F32)
        terms.append((0 if index == 1 else 2, weight[heads : 2 * heads] * grown * keep))
    if index & 2:
        keep = (docs[first + 1] == docs[first + index]).astype(F32)
        factor = grown
        if index == 3:
            factor = grown * jnp.exp(jnp.concatenate([previous, previous], axis=1))
        terms.append((1, weight[2 * heads : 3 * heads] * factor * keep))
    crosses = [(dot_nt(local[slot], c_out), row) for slot, row in terms]
    for h in range(heads):
        at = slice(h * HEAD, (h + 1) * HEAD)
        col = cum_col[:, h : h + 1]
        row = cum[h : h + 1, :]

        def block(s, t, masked):
            decay = jnp.exp(
                jnp.broadcast_to(row[:, t * 128 : t * 128 + 128], (128, 128)) - col[s * 128 : s * 128 + 128, :]
            )
            if masked:
                decay = jnp.where(causal, decay, 0.0)
            return (scores[s * 128 : s * 128 + 128, t * 128 : t * 128 + 128] * decay).astype(BF16)

        vh = v[pl.ds(h * HEAD, HEAD), :]
        left = dot(vh[:, :128], block(0, 0, True))
        right = dot(vh, jnp.concatenate([block(0, 1, False), block(1, 1, True)], axis=0))
        out = skip[h] * vh.astype(F32) + weight[h : h + 1, :] * jnp.concatenate([left, right], axis=1)
        for cross, factor in crosses:
            out = out + factor[h : h + 1, :] * cross[at]
        ho_out[pl.ds(h * HEAD, HEAD), :] = out


def intra(index, meta, docs, skip, tokens, w_gate, w_level, v, sp, log_decay, local, start):
    depth = tokens.shape[1]
    heads = log_decay.shape[1]
    width = w_gate.shape[1]
    smem = pl.BlockSpec(memory_space=pltpu.SMEM)
    whole = lambda shape: pl.BlockSpec(shape, lambda i: (0,) * len(shape))
    return pl.pallas_call(
        functools.partial(intra_kernel, index),
        name=f"intra{index}",
        grid=(1,),
        in_specs=[
            smem,
            smem,
            smem,
            pl.BlockSpec((STRETCH, depth), lambda i: (index, 0)),
            whole((depth, width)),
            whole((depth, heads * LEVELS)),
            pl.BlockSpec((pl.Squeezed(), width, STRETCH), lambda i: (index, 0, 0)),
            pl.BlockSpec((STRETCH, 2 * STATE), lambda i: (index, 0)),
            pl.BlockSpec((STRETCH, heads), lambda i: (index, 0)),
            whole((3, width, STATE)),
            whole((2 * heads, STATE)),
        ],
        out_specs=[
            whole((width, STRETCH)),
            whole((width, STRETCH)),
            whole((heads * LEVELS, STRETCH)),
            whole((2 * heads, STATE)),
        ],
        out_shape=[
            jax.ShapeDtypeStruct((width, STRETCH), BF16),
            jax.ShapeDtypeStruct((width, STRETCH), F32),
            jax.ShapeDtypeStruct((heads * LEVELS, STRETCH), F32),
            jax.ShapeDtypeStruct((2 * heads, STATE), F32),
        ],
        compiler_params=pltpu.CompilerParams(vmem_limit_bytes=VMEM_BYTES),
        cost_estimate=pl.CostEstimate(
            flops=2 * STRETCH * depth * (width + STATE) * 2,
            bytes_accessed=2 * (STRETCH * depth + depth * width),
            transcendentals=0,
        ),
    )(meta, docs, skip, tokens, w_gate, w_level, v, sp, log_decay, local, start)


def finish_kernel(count, index, meta, docs, gain, w_out, sp, *refs):
    gates, hos, lws = refs[:count], refs[count : 2 * count], refs[2 * count : 3 * count]
    refs = refs[3 * count :]
    near, owns, swaps, earliers = refs[0], refs[1:5], refs[5:9], refs[9:13]
    plus_out, minus_out, keep_out, own_out, acc, turned = refs[13:]
    ctx, tp = meta[0], meta[1]
    core = ctx & 1
    heads = earliers[0].shape[0]
    half = heads // 2
    for j in range(count):
        stretch_doc = docs[ctx * 4 + index + j]
        c_out = sp[pl.ds(j * STRETCH, STRETCH), STATE:]
        acc[...] = hos[j][...]
        for bit in range(5):
            base = (ctx >> (bit + 1)) << (bit + 1)
            last_left = docs[(base + (1 << bit)) * 4 - 1]
            live = ((((ctx >> bit) & 1) == 1) & (last_left == stretch_doc)).astype(F32)
            rows = lws[j][pl.ds((bit + 3) * heads, heads), :] * live
            if bit == 0:
                cross = dot_nt(near[pl.ds(0, heads * HEAD), :], c_out)
                for h in range(heads):
                    at = pl.ds(h * HEAD, HEAD)
                    acc[at, :] = acc[at, :] + rows[h : h + 1, :] * cross[h * HEAD : (h + 1) * HEAD]
                continue
            factor = jnp.exp(earliers[bit - 1][...])
            turned_rows = rows * jnp.concatenate([factor, factor], axis=1)
            lower, upper = turned_rows[:half], turned_rows[half:]
            mine = jnp.where(core == 0, lower, upper)
            other = jnp.where(core == 0, upper, lower)
            for source, row, part in ((owns[bit - 1], mine, core), (swaps[bit - 1], other, 1 - core)):
                cross = dot_nt(source[pl.ds(0, half * HEAD), :], c_out)
                for h in range(half):
                    at = pl.ds(pl.multiple_of(part * (half * HEAD) + h * HEAD, HEAD), HEAD)
                    acc[at, :] = acc[at, :] + row[h : h + 1, :] * cross[h * HEAD : (h + 1) * HEAD]
        for h in range(heads):
            at = pl.ds(h * HEAD, HEAD)
            g = gates[j][at, :].astype(F32)
            gated = acc[at, :] * (g / (1.0 + jnp.exp(-g)))
            power = jnp.sum(gated * gated, axis=0, keepdims=True) * (1.0 / HEAD)
            turned[at, :] = (gated * lax.rsqrt(power + 1e-5) * gain[at, :]).astype(BF16)
        normed = jnp.transpose(turned[...])
        quarter = w_out.shape[1] // 8
        here = pl.ds(j * STRETCH, STRETCH)

        def piece(shift, side):
            col = pl.multiple_of((((tp + shift) & 3) * 2 + side) * quarter, quarter)
            return dot(normed, w_out[:, pl.ds(col, quarter)]).astype(BF16)

        first, second = pl.ds(0, quarter), pl.ds(quarter, quarter)
        plus_out[here, first] = piece(2, 0)
        plus_out[here, second] = piece(1, 1)
        minus_out[here, first] = piece(2, 1)
        minus_out[here, second] = piece(3, 0)
        keep_out[here, first] = piece(1, 0)
        keep_out[here, second] = piece(3, 1)
        own_out[here, first] = piece(0, 0)
        own_out[here, second] = piece(0, 1)


def finish(start, stop, meta, docs, gain, w_out, sp, gates, hos, lws, near, owns, swaps, earliers):
    count = stop - start
    width, depth = w_out.shape
    heads = earliers[0].shape[0]
    rows = count * STRETCH
    smem = pl.BlockSpec(memory_space=pltpu.SMEM)
    vmem = pl.BlockSpec(memory_space=pltpu.VMEM)
    whole = lambda shape: pl.BlockSpec(shape, lambda i: (0,) * len(shape))
    operands = [*gates, *hos, *lws, near, *owns, *swaps, *earliers]
    return pl.pallas_call(
        functools.partial(finish_kernel, count, start),
        name=f"finish{start}",
        grid=(1,),
        in_specs=[
            smem,
            smem,
            whole(gain.shape),
            whole(w_out.shape),
            pl.BlockSpec((rows, 2 * STATE), lambda i: (start // count, 0)),
            *[whole(x.shape) for x in operands],
        ],
        out_specs=[whole((rows, depth // 4))] * 4,
        out_shape=[jax.ShapeDtypeStruct((rows, depth // 4), BF16)] * 4,
        scratch_shapes=[pltpu.VMEM((width, STRETCH), F32), pltpu.VMEM((width, STRETCH), BF16)],
        compiler_params=pltpu.CompilerParams(vmem_limit_bytes=VMEM_BYTES),
        cost_estimate=pl.CostEstimate(
            flops=4 * rows * depth * width, bytes_accessed=2 * width * depth + 8 * rows * width, transcendentals=0
        ),
    )(meta, docs, gain, w_out, sp, *operands)


def per_device(tokens, w_value, w_gate, w_state, w_level, log_decay, skip_weight, norm_gain, doc_ids, w_out):
    heads = log_decay.shape[1]
    steps = tokens.shape[0] // STRETCH
    ctx, tp = lax.axis_index("ctx"), lax.axis_index("tp")
    meta = jnp.where(jnp.arange(2, dtype=jnp.int32) == 0, ctx, tp)
    v, sp, local, pay = project(meta, doc_ids, tokens, w_value, w_state, log_decay)

    def across(x, bit):
        return lax.ppermute(x, "ctx", [(i, i ^ (1 << bit)) for i in range(32)])

    def turn(x, by):
        return lax.ppermute(x, "tp", [(i, (i + by) % 4) for i in range(4)])

    gain = norm_gain.reshape(-1, 1)
    earlier = jnp.zeros((heads, STATE), F32)
    start = jnp.zeros((2 * heads, STATE), F32)
    near, owns, swaps, earliers, gates, hos, lws = None, [], [], [], [], [], []
    for bit in range(5):
        peer = across(pay, bit)
        if bit == 0:
            near = peer
        else:
            owns.append(peer)
            swaps.append(across(peer, 0))
            g, ho, lw, start = intra(
                bit - 1, meta, doc_ids, skip_weight, tokens, w_gate, w_level, v, sp, log_decay, local, start
            )
            gates.append(g)
            hos.append(ho)
            lws.append(lw)
        if bit < 4:
            pay, earlier = combine(bit, meta, doc_ids, pay, peer, earlier, half=bit > 0)
            earliers.append(earlier)
    results = []
    half = w_out.shape[1] // 8
    for lo, hi in CHUNKS:
        plus, minus, keep, own = finish(
            lo, hi, meta, doc_ids, gain, w_out, sp, gates[lo:hi], hos[lo:hi], lws[lo:hi], near, owns, swaps, earliers
        )
        from_below, from_above = turn(plus, 1), turn(minus, 3)
        on_plus = (keep[:, :half].astype(F32) + from_below[:, :half].astype(F32)).astype(BF16)
        on_minus = (keep[:, half:].astype(F32) + from_above[:, :half].astype(F32)).astype(BF16)
        last_below, last_above = turn(on_plus, 1), turn(on_minus, 3)
        left = own[:, :half].astype(F32) + from_above[:, half:].astype(F32) + last_below.astype(F32)
        right = own[:, half:].astype(F32) + from_below[:, half:].astype(F32) + last_above.astype(F32)
        results.append(jnp.concatenate([left, right], axis=1).astype(BF16))
    return jnp.concatenate(results, axis=0)


def solution(mesh):
    placed = (
        P("ctx", None),
        P(None, "tp"),
        P(None, "tp"),
        P(),
        P(None, "tp"),
        P("ctx", "tp"),
        P("tp"),
        P("tp"),
        P(),
        P("tp", None),
    )
    return jax.shard_map(per_device, mesh=mesh, in_specs=placed, out_specs=P("ctx", "tp"), check_vma=False)
```

```python
import functools

import jax
import jax.numpy as jnp
from jax import lax
from jax.experimental import pallas as pl
from jax.experimental.pallas import tpu as pltpu
from jax.sharding import PartitionSpec as P

STRETCH = 256
STEPS = 4
HEAD = 64
STATE = 128
LEVELS = 8
BLOCK = 256
F32 = jnp.float32
BF16 = jnp.bfloat16
HIGHEST = lax.Precision.HIGHEST
NT = (((1,), (1,)), ((), ()))
CHUNKS = ((0, 2), (2, 4))
SMEM = pl.BlockSpec(memory_space=pltpu.SMEM)
VMEM = pl.BlockSpec(memory_space=pltpu.VMEM)
FAR = pl.BlockSpec(memory_space=pltpu.HBM)


def dot(a, b):
    return jnp.dot(a, b, preferred_element_type=F32)


def dot_nt(a, b):
    return lax.dot_general(a, b, NT, preferred_element_type=F32)


def iota(shape, dim):
    return lax.broadcasted_iota(jnp.int32, shape, dim)


def far(x):
    return pltpu.with_memory_space_constraint(x, pltpu.HBM)


def twice(x):
    return jnp.concatenate([x, x], axis=1)


def upper_ones():
    shape = (STRETCH, STRETCH)
    return (iota(shape, 0) <= iota(shape, 1)).astype(F32)


def running_sums(decays):
    return jnp.dot(decays, upper_ones(), precision=HIGHEST, preferred_element_type=F32)


def lanes(column):
    return jnp.broadcast_to(column, (column.shape[0], STATE))


def store_total(ref, top, total):
    heads = total.shape[0]
    high = total.astype(BF16)
    rest = total - high.astype(F32)
    middle = rest.astype(BF16)
    low = (rest - middle.astype(F32)).astype(BF16)
    ref[pl.ds(top, heads), :] = high
    ref[pl.ds(top + heads, heads), :] = middle
    ref[pl.ds(top + 2 * heads, heads), :] = low


def load_total(ref, top, heads):
    parts = [ref[pl.ds(top + k * heads, heads), :].astype(F32) for k in range(3)]
    return (parts[0] + parts[1]) + parts[2]


def call(kernel, name, in_specs, out_shape, args, scratch=(), mib=8, flops=1 << 20, moved=1 << 20, out_specs=None):
    return pl.pallas_call(
        kernel,
        name=name,
        in_specs=in_specs,
        out_specs=[VMEM] * len(out_shape),
        out_shape=[jax.ShapeDtypeStruct(*x) for x in out_shape],
        scratch_shapes=list(scratch),
        compiler_params=pltpu.CompilerParams(vmem_limit_bytes=mib << 20),
        cost_estimate=pl.CostEstimate(flops=flops, bytes_accessed=moved, transcendentals=0),
    )(*args)


def project_kernel(
    meta, docs, decays, tok_hbm, value_hbm, state_hbm, gate_hbm, tok, gate, sp, v, local, pay, w_value, w_state, tail,
    grow, scaled, sems,
):
    heads = decays.shape[0]
    blocks = w_value.shape[1] // BLOCK
    per_block = BLOCK // HEAD

    def token_copy(i):
        at = pl.ds(i * STRETCH, STRETCH)
        return pltpu.make_async_copy(tok_hbm.at[at, :], tok.at[at, :], sems.at[i])

    def value_copy(k):
        at = pl.ds(pl.multiple_of(k * BLOCK, BLOCK), BLOCK)
        return pltpu.make_async_copy(value_hbm.at[:, at], w_value.at[:, at], sems.at[STEPS + k])

    state_copy = pltpu.make_async_copy(state_hbm, w_state, sems.at[STEPS + blocks])
    gate_copy = pltpu.make_async_copy(gate_hbm, gate, sems.at[STEPS + blocks + 1])
    token_copy(0).start()
    state_copy.start()
    for i in range(1, STEPS):
        token_copy(i).start()
    value_copy(0).start()

    stacked = jnp.concatenate([decays[:, i * STRETCH : (i + 1) * STRETCH] for i in range(STEPS)], axis=0)
    cum = running_sums(stacked)
    total = lanes(cum[:, STRETCH - 1 :])
    rest = jnp.exp(twice(total) - cum)
    first = meta[0] * STEPS
    whole = jnp.zeros((heads, STATE), F32)
    for i in range(STEPS):
        rows = slice(i * heads, (i + 1) * heads)
        tail[:, pl.ds(i * STRETCH, STRETCH)] = rest[rows]
        same = (docs[first + max(i - 1, 0)] == docs[first + i]).astype(F32)
        grow[i] = jnp.exp(total[rows]) * same
        whole = whole + total[rows]
    store_total(pay, heads * HEAD, whole)

    state_copy.wait()
    for i in range(STEPS):
        token_copy(i).wait()
        at = pl.ds(i * STRETCH, STRETCH)
        sp[at, :] = dot(tok[at, :], w_state[...]).astype(BF16)

    @pl.loop(0, blocks)
    def _(k):
        value_copy(k).wait()

        @pl.when(k + 1 < blocks)
        def _():
            value_copy(k + 1).start()

        @pl.when(k == 1)
        def _():
            gate_copy.start()

        at = pl.ds(pl.multiple_of(k * BLOCK, BLOCK), BLOCK)
        v[at, :] = jnp.transpose(dot(tok[...], w_value[:, at]).astype(BF16))
        for h in range(per_block):
            rows = pl.ds(pl.multiple_of(k * BLOCK + h * HEAD, HEAD), HEAD)
            scaled[pl.ds(h * HEAD, HEAD), :] = (
                v[rows, :].astype(F32) * tail[pl.ds(k * per_block + h, 1), :]
            ).astype(BF16)
        run = None
        for i in range(STEPS):
            here = pl.ds(i * STRETCH, STRETCH)
            state = dot(scaled[:, here], sp[here, :STATE])
            if i == 0:
                run = state
                local[0, at, :] = state.astype(BF16)
                continue
            factor = jnp.concatenate(
                [
                    jnp.broadcast_to(grow[i, pl.ds(k * per_block + h, 1), :], (HEAD, STATE))
                    for h in range(per_block)
                ],
                axis=0,
            )
            run = run * factor + state
            if i == 1:
                local[1, at, :] = run.astype(BF16)
            if i == 2:
                local[2, at, :] = state.astype(BF16)
        pay[at, :] = run.astype(BF16)

    gate_copy.wait()


def project(meta, docs, decays, tokens, w_value, w_state, w_gate):
    rows, depth = tokens.shape
    heads = decays.shape[0]
    width = w_value.shape[1]
    return call(
        project_kernel,
        "project",
        [SMEM, SMEM, VMEM, FAR, FAR, FAR, FAR],
        [
            ((rows, depth), BF16),
            ((depth, width), BF16),
            ((rows, 2 * STATE), BF16),
            ((width, rows), BF16),
            ((3, width, STATE), BF16),
            ((width + 3 * heads, STATE), BF16),
        ],
        (meta, docs, decays, *(far(x) for x in (tokens, w_value, w_state, w_gate))),
        [
            pltpu.VMEM((depth, width), BF16),
            pltpu.VMEM((depth, 2 * STATE), BF16),
            pltpu.VMEM((heads, rows), F32),
            pltpu.VMEM((STEPS, heads, STATE), F32),
            pltpu.VMEM((BLOCK, rows), BF16),
            pltpu.SemaphoreType.DMA((STEPS + width // BLOCK + 2,)),
        ],
        mib=16,
        flops=2 * rows * depth * (width + 2 * STATE),
        moved=2 * (rows * depth + 2 * depth * width),
    )


def joined(docs, last_first, last_second):
    return (docs[last_first] == docs[last_second]).astype(F32)


def near_kernel(meta, docs, own, peer, pay, earlier):
    heads = earlier.shape[0]
    top = heads * HEAD
    ctx = meta[0]
    second = (ctx & 1) == 1
    pair = ctx >> 1
    total_own, total_peer = load_total(own, top, heads), load_total(peer, top, heads)
    keep = joined(docs, pair * 2 * STEPS + STEPS - 1, pair * 2 * STEPS + 2 * STEPS - 1)
    factor = jnp.exp(jnp.where(second, total_own, total_peer)) * keep
    own_by = jnp.where(second, 1.0, factor)
    peer_by = jnp.where(second, factor, 1.0)
    for h in range(heads):
        at = pl.ds(h * HEAD, HEAD)
        pay[at, :] = (own[at, :].astype(F32) * own_by[h : h + 1] + peer[at, :].astype(F32) * peer_by[h : h + 1]).astype(
            BF16
        )
    store_total(pay, top, total_own + total_peer)
    earlier[...] = jnp.where(second, total_peer, 0.0)


def middle_kernel(meta, docs, own, one, two, three, before, pay, left, earlier):
    heads = before.shape[0]
    top = heads * HEAD
    ctx = meta[0]
    chip = ctx >> 1
    odd, high = (chip & 1) == 1, (chip & 2) == 2
    t_own, t_one, t_two, t_three = (load_total(x, top, heads) for x in (own, one, two, three))
    last = lambda at: (at + 1) * 2 * STEPS - 1
    base, mine, theirs = (chip >> 2) << 2, (chip >> 1) << 1, ((chip >> 1) ^ 1) << 1
    keep_mine = joined(docs, last(mine), last(mine + 1))
    keep_theirs = joined(docs, last(theirs), last(theirs + 1))
    keep_all = joined(docs, last(base + 1), last(base + 3))
    by_mine = jnp.exp(jnp.where(odd, t_own, t_one)) * keep_mine
    by_theirs = jnp.exp(jnp.where(odd, t_two, t_three)) * keep_theirs
    own_by, one_by = jnp.where(odd, 1.0, by_mine), jnp.where(odd, by_mine, 1.0)
    two_by, three_by = jnp.where(odd, 1.0, by_theirs), jnp.where(odd, by_theirs, 1.0)
    by_all = jnp.exp(jnp.where(high, t_own + t_one, t_two + t_three)) * keep_all
    mine_by, theirs_by = jnp.where(high, 1.0, by_all), jnp.where(high, by_all, 1.0)
    for h in range(heads):
        at = pl.ds(h * HEAD, HEAD)
        row = slice(h, h + 1)
        here = own[at, :].astype(F32) * own_by[row] + one[at, :].astype(F32) * one_by[row]
        there = two[at, :].astype(F32) * two_by[row] + three[at, :].astype(F32) * three_by[row]
        left[at, :] = there.astype(BF16)
        pay[at, :] = (here * mine_by[row] + there * theirs_by[row]).astype(BF16)
    store_total(pay, top, (t_own + t_one) + (t_two + t_three))
    second = before[...] + jnp.where(odd, t_one, 0.0)
    earlier[pl.ds(0, heads), :] = second
    earlier[pl.ds(heads, heads), :] = second + jnp.where(high, t_two + t_three, 0.0)


def far_kernel(meta, docs, one, two, three, before, left, earlier):
    heads = earlier.shape[0]
    top = heads * HEAD
    row_of = meta[0] >> 3
    odd = (row_of & 1) == 1
    t_one, t_two, t_three = (load_total(x, top, heads) for x in (one, two, three))
    theirs = ((row_of >> 1) ^ 1) << 1
    last = lambda at: (at + 1) * 8 * STEPS - 1
    factor = jnp.exp(jnp.where(odd, t_two, t_three)) * joined(docs, last(theirs), last(theirs + 1))
    two_by, three_by = jnp.where(odd, 1.0, factor), jnp.where(odd, factor, 1.0)
    for h in range(heads):
        at = pl.ds(h * HEAD, HEAD)
        left[at, :] = (
            two[at, :].astype(F32) * two_by[h : h + 1] + three[at, :].astype(F32) * three_by[h : h + 1]
        ).astype(BF16)
    earlier[...] = before[pl.ds(heads, heads), :] + jnp.where(odd, t_one, 0.0)


def gate_kernel(tok, gate, w_level, out_hbm, gates, weight, w_out, sem):
    copy = pltpu.make_async_copy(out_hbm, w_out, sem)
    copy.start()
    cols = w_level.shape[1]
    heads = cols // LEVELS
    to_row, from_col = iota((cols, cols), 0), iota((cols, cols), 1)
    pick = ((to_row % heads) * LEVELS + to_row // heads == from_col).astype(BF16)
    turned = dot_nt(pick, dot(tok[...], w_level[...]).astype(BF16))
    weight[...] = jnp.maximum(turned, 0.0) + jnp.log1p(jnp.exp(-jnp.abs(turned)))

    @pl.loop(0, gate.shape[1] // BLOCK)
    def _(k):
        at = pl.ds(pl.multiple_of(k * BLOCK, BLOCK), BLOCK)
        gates[at, :] = jnp.transpose(dot(tok[...], gate[:, at]).astype(BF16))

    copy.wait()


def intra_kernel(meta, docs, skip, weight, decays, v, sp, local, ho, scaled_weight):
    heads = decays.shape[0]
    first = meta[0] * STEPS
    causal = iota((128, 128), 0) <= iota((128, 128), 1)
    lower = (iota((STRETCH, STRETCH), 0) >= iota((STRETCH, STRETCH), 1)).astype(F32)
    begin = jnp.zeros((heads, STATE), F32)
    previous = begin
    for index in range(STEPS):
        here = pl.ds(index * STRETCH, STRETCH)
        now = decays[:, here]
        cum = running_sums(now)
        cum_col = lax.dot_general(lower, now, NT, precision=HIGHEST, preferred_element_type=F32)
        total = lanes(cum[:, STRETCH - 1 :])
        grown = jnp.exp(cum)
        from_device = jnp.exp(cum + twice(begin))
        for level in range(3, LEVELS):
            rows = pl.ds(level * heads, heads)
            scaled_weight[rows, here] = weight[rows, here] * from_device
        b_in, c_out = sp[here, :STATE], sp[here, STATE:]
        scores = dot_nt(b_in, c_out)
        terms = []
        if index & 1:
            keep = joined(docs, first + index - 1, first + index)
            terms.append((0 if index == 1 else 2, weight[pl.ds(heads, heads), here] * grown * keep))
        if index & 2:
            keep = joined(docs, first + 1, first + index)
            factor = grown * jnp.exp(twice(previous)) if index == 3 else grown
            terms.append((1, weight[pl.ds(2 * heads, heads), here] * factor * keep))
        crosses = [(dot_nt(local[slot], c_out), row) for slot, row in terms]
        own_weight = weight[pl.ds(0, heads), here]
        for h in range(heads):
            at = slice(h * HEAD, (h + 1) * HEAD)
            col = cum_col[:, h : h + 1]
            row = cum[h : h + 1, :]

            def block(s, t, masked):
                decay = jnp.exp(
                    jnp.broadcast_to(row[:, t * 128 : t * 128 + 128], (128, 128)) - col[s * 128 : s * 128 + 128, :]
                )
                if masked:
                    decay = jnp.where(causal, decay, 0.0)
                return (scores[s * 128 : s * 128 + 128, t * 128 : t * 128 + 128] * decay).astype(BF16)

            vh = v[pl.ds(h * HEAD, HEAD), here]
            left = dot(vh[:, :128], block(0, 0, True))
            right = dot(vh, jnp.concatenate([block(0, 1, False), block(1, 1, True)], axis=0))
            out = skip[h] * vh.astype(F32) + own_weight[h : h + 1, :] * jnp.concatenate([left, right], axis=1)
            for cross, factor in crosses:
                out = out + factor[h : h + 1, :] * cross[at]
            ho[pl.ds(h * HEAD, HEAD), here] = out
        begin = begin + total
        previous = total


def finish_kernel(
    start, count, meta, docs, gain, w_out, sp, gates, ho, weight, e1, e23, e4, *refs
):
    sources = refs[:5]
    plus, minus, keep, own, acc, normed = refs[5:]
    ctx, tp = meta[0], meta[1]
    heads = e1.shape[0]
    for j in range(count):
        here = pl.ds((start + j) * STRETCH, STRETCH)
        stretch_doc = docs[ctx * STEPS + start + j]
        c_out = sp[here, STATE:]
        terms = []
        for bit in range(5):
            base = (ctx >> (bit + 1)) << (bit + 1)
            last_left = docs[(base + (1 << bit)) * STEPS - 1]
            live = ((((ctx >> bit) & 1) == 1) & (last_left == stretch_doc)).astype(F32)
            rows = weight[pl.ds((bit + 3) * heads, heads), here] * live
            if bit:
                gone = (None, e1[...], e23[pl.ds(0, heads), :], e23[pl.ds(heads, heads), :], e4[...])[bit]
                rows = rows * twice(jnp.exp(gone))
            terms.append((dot_nt(sources[bit][pl.ds(0, heads * HEAD), :], c_out), rows))
        for h in range(heads):
            at = pl.ds(h * HEAD, HEAD)
            total = ho[at, here]
            for cross, rows in terms:
                total = total + rows[h : h + 1, :] * cross[h * HEAD : (h + 1) * HEAD]
            g = gates[at, here].astype(F32)
            gated = total * (g / (1.0 + jnp.exp(-g)))
            power = jnp.sum(gated * gated, axis=0, keepdims=True) * (1.0 / HEAD)
            acc[at, :] = gated * lax.rsqrt(power + 1e-5)
        normed[pl.ds(j * STRETCH, STRETCH), :] = (jnp.transpose(acc[...]) * gain[...]).astype(BF16)
    quarter = w_out.shape[1] // 8

    def piece(shift, side):
        col = pl.multiple_of((((tp + shift) & 3) * 2 + side) * quarter, quarter)
        return dot(normed[...], w_out[:, pl.ds(col, quarter)]).astype(BF16)

    first, second = pl.ds(0, quarter), pl.ds(quarter, quarter)
    plus[:, first] = piece(2, 0)
    plus[:, second] = piece(1, 1)
    minus[:, first] = piece(2, 1)
    minus[:, second] = piece(3, 0)
    keep[:, first] = piece(1, 0)
    keep[:, second] = piece(3, 1)
    own[:, first] = piece(0, 0)
    own[:, second] = piece(0, 1)


def finish(start, stop, meta, docs, gain, w_out, *operands):
    count = stop - start
    width, depth = w_out.shape
    rows = count * STRETCH
    return call(
        functools.partial(finish_kernel, start, count),
        f"finish{start}",
        [SMEM] * 2 + [VMEM] * (2 + len(operands)),
        [((rows, depth // 4), BF16)] * 4,
        (meta, docs, gain, w_out, *operands),
        [pltpu.VMEM((width, STRETCH), F32), pltpu.VMEM((rows, width), BF16)],
        mib=16,
        flops=4 * rows * depth * width,
        moved=2 * width * depth + 8 * rows * width,
    )


def per_device(tokens, w_value, w_gate, w_state, w_level, log_decay, skip_weight, norm_gain, doc_ids, w_out):
    rows, depth = tokens.shape
    width = w_value.shape[1]
    heads = log_decay.shape[1]
    ctx, tp = lax.axis_index("ctx"), lax.axis_index("tp")
    meta = jnp.where(jnp.arange(2, dtype=jnp.int32) == 0, ctx, tp)
    decays = jnp.transpose(log_decay)
    payload = ((width + 3 * heads, STATE), BF16)
    tail = ((width, STATE), BF16)

    def across(x, by):
        return lax.ppermute(x, "ctx", [(i, i ^ by) for i in range(32)])

    def upward(x, by):
        return lax.ppermute(x, "ctx", [(i, i ^ by) for i in range(32) if i < i ^ by])

    def turn(x, by):
        return lax.ppermute(x, "tp", [(i, (i + by) % 4) for i in range(4)])

    tok, gate, sp, v, local, pay0 = project(meta, doc_ids, decays, tokens, w_value, w_state, w_gate)
    peer = across(pay0, 1)
    pay1, e1 = call(
        near_kernel, "near", [SMEM] * 2 + [VMEM] * 2, [payload, ((heads, STATE), F32)], (meta, doc_ids, pay0, peer)
    )
    ys = [across(pay1, by) for by in (4, 2, 6)]
    gates, weight, w_out_near = call(
        gate_kernel,
        "gate",
        [VMEM] * 3 + [FAR],
        [((width, rows), BF16), ((heads * LEVELS, rows), F32), (w_out.shape, BF16)],
        (tok, gate, w_level, far(w_out)),
        [pltpu.SemaphoreType.DMA(())],
        mib=12,
        flops=2 * rows * depth * (width + STATE),
        moved=2 * (rows * depth + depth * width),
    )
    y2, y1, y3 = ys
    pay2, left2, e23 = call(
        middle_kernel,
        "middle",
        [SMEM] * 2 + [VMEM] * 5,
        [payload, tail, ((2 * heads, STATE), F32)],
        (meta, doc_ids, pay1, y1, y2, y3, e1),
    )
    x2, x1, x3 = (upward(pay2, by) for by in (16, 8, 24))
    ho, scaled_weight = call(
        intra_kernel,
        "intra",
        [SMEM] * 3 + [VMEM] * 5,
        [((width, rows), F32), ((heads * LEVELS, rows), F32)],
        (meta, doc_ids, skip_weight, weight, decays, v, sp, local),
        mib=12,
        flops=6 << 30,
        moved=8 << 20,
    )
    left4, e4 = call(
        far_kernel,
        "far",
        [SMEM] * 2 + [VMEM] * 4,
        [tail, ((heads, STATE), F32)],
        (meta, doc_ids, x1, x2, x3, e23),
    )
    gain = norm_gain.reshape(1, -1)
    results = []
    half = w_out.shape[1] // 8
    for lo, hi in CHUNKS:
        plus, minus, keep, own = finish(
            lo, hi, meta, doc_ids, gain, w_out_near, sp, gates, ho, scaled_weight, e1, e23, e4, peer, y1, left2, x1, left4
        )
        from_below, from_above = turn(plus, 1), turn(minus, 3)
        on_plus = (keep[:, :half].astype(F32) + from_below[:, :half].astype(F32)).astype(BF16)
        on_minus = (keep[:, half:].astype(F32) + from_above[:, :half].astype(F32)).astype(BF16)
        last_below, last_above = turn(on_plus, 1), turn(on_minus, 3)
        first = own[:, :half].astype(F32) + from_above[:, half:].astype(F32) + last_below.astype(F32)
        second = own[:, half:].astype(F32) + from_below[:, half:].astype(F32) + last_above.astype(F32)
        results.append(jnp.concatenate([first, second], axis=1).astype(BF16))
    return jnp.concatenate(results, axis=0)


def solution(mesh):
    placed = (
        P("ctx", None),
        P(None, "tp"),
        P(None, "tp"),
        P(),
        P(None, "tp"),
        P("ctx", "tp"),
        P("tp"),
        P("tp"),
        P(),
        P("tp", None),
    )
    return jax.shard_map(per_device, mesh=mesh, in_specs=placed, out_specs=P("ctx", "tp"), check_vma=False)
```

```python
import functools

import jax
import jax.numpy as jnp
from jax import lax
from jax.experimental import pallas as pl
from jax.experimental.pallas import tpu as pltpu
from jax.sharding import PartitionSpec as P

STRETCH = 256
STEPS = 4
HEAD = 64
STATE = 128
LEVELS = 8
BLOCK = 256
F32 = jnp.float32
BF16 = jnp.bfloat16
HIGHEST = lax.Precision.HIGHEST
NT = (((1,), (1,)), ((), ()))
CHUNKS = ((0, 2), (2, 4))
SMEM = pl.BlockSpec(memory_space=pltpu.SMEM)
VMEM = pl.BlockSpec(memory_space=pltpu.VMEM)
FAR = pl.BlockSpec(memory_space=pltpu.HBM)


def dot(a, b):
    return jnp.dot(a, b, preferred_element_type=F32)


def dot_nt(a, b):
    return lax.dot_general(a, b, NT, preferred_element_type=F32)


def iota(shape, dim):
    return lax.broadcasted_iota(jnp.int32, shape, dim)


def far(x):
    return pltpu.with_memory_space_constraint(x, pltpu.HBM)


def twice(x):
    return jnp.concatenate([x, x], axis=1)


def upper_ones():
    shape = (STRETCH, STRETCH)
    return (iota(shape, 0) <= iota(shape, 1)).astype(F32)


def running_sums(decays):
    return jnp.dot(decays, upper_ones(), precision=HIGHEST, preferred_element_type=F32)


def lanes(column):
    return jnp.broadcast_to(column, (column.shape[0], STATE))


def store_total(ref, top, total):
    heads = total.shape[0]
    high = total.astype(BF16)
    rest = total - high.astype(F32)
    middle = rest.astype(BF16)
    low = (rest - middle.astype(F32)).astype(BF16)
    ref[pl.ds(top, heads), :] = high
    ref[pl.ds(top + heads, heads), :] = middle
    ref[pl.ds(top + 2 * heads, heads), :] = low


def load_total(ref, top, heads):
    parts = [ref[pl.ds(top + k * heads, heads), :].astype(F32) for k in range(3)]
    return (parts[0] + parts[1]) + parts[2]


def call(kernel, name, in_specs, out_shape, args, scratch=(), mib=8, flops=1 << 20, moved=1 << 20, out_specs=None):
    return pl.pallas_call(
        kernel,
        name=name,
        in_specs=in_specs,
        out_specs=[VMEM] * len(out_shape),
        out_shape=[jax.ShapeDtypeStruct(*x) for x in out_shape],
        scratch_shapes=list(scratch),
        compiler_params=pltpu.CompilerParams(vmem_limit_bytes=mib << 20),
        cost_estimate=pl.CostEstimate(flops=flops, bytes_accessed=moved, transcendentals=0),
    )(*args)


def project_kernel(
    docs, decays_hbm, tok_hbm, value_hbm, state_hbm, tok, sp, v, local, pay, w_value, w_state, tail, grow, scaled, decays,
    sems,
):
    heads = decays.shape[0]
    blocks = w_value.shape[1] // BLOCK
    per_block = BLOCK // HEAD

    def token_copy(i):
        at = pl.ds(i * STRETCH, STRETCH)
        return pltpu.make_async_copy(tok_hbm.at[at, :], tok.at[at, :], sems.at[i])

    def value_copy(k):
        at = pl.ds(k * BLOCK, BLOCK)
        return pltpu.make_async_copy(value_hbm.at[:, at], w_value.at[:, at], sems.at[STEPS + k])

    state_copy = pltpu.make_async_copy(state_hbm, w_state, sems.at[STEPS + blocks])
    decay_copy = pltpu.make_async_copy(decays_hbm, decays, sems.at[STEPS + blocks + 1])
    decay_copy.start()
    token_copy(0).start()
    state_copy.start()
    value_copy(0).start()
    for i in range(1, STEPS):
        token_copy(i).start()
    value_copy(1).start()

    decay_copy.wait()
    stacked = jnp.concatenate([decays[:, pl.ds(i * STRETCH, STRETCH)] for i in range(STEPS)], axis=0)
    cum = running_sums(stacked)
    total = lanes(cum[:, STRETCH - 1 :])
    rest = jnp.exp(twice(total) - cum)
    first = lax.axis_index("ctx") * STEPS
    whole = jnp.zeros((heads, STATE), F32)
    for i in range(STEPS):
        rows = slice(i * heads, (i + 1) * heads)
        tail[:, pl.ds(i * STRETCH, STRETCH)] = rest[rows]
        same = (docs[first + max(i - 1, 0)] == docs[first + i]).astype(F32)
        grow[i] = jnp.exp(total[rows]) * same
        whole = whole + total[rows]
    store_total(pay, heads * HEAD, whole)

    def states(k):
        at = pl.ds(k * BLOCK, BLOCK)
        for h in range(per_block):
            rows = pl.ds(k * BLOCK + h * HEAD, HEAD)
            row = k * per_block + h
            scaled[rows, :] = (v[rows, :].astype(F32) * tail[row : row + 1, :]).astype(BF16)
        run = None
        for i in range(STEPS):
            here = pl.ds(i * STRETCH, STRETCH)
            state = dot(scaled[at, here], sp[here, :STATE])
            if i == 0:
                run = state
                local[0, at, :] = state.astype(BF16)
                continue
            factor = jnp.concatenate(
                [
                    jnp.broadcast_to(grow[i, k * per_block + h : k * per_block + h + 1, :], (HEAD, STATE))
                    for h in range(per_block)
                ],
                axis=0,
            )
            run = run * factor + state
            if i == 1:
                local[1, at, :] = run.astype(BF16)
            if i == 2:
                local[2, at, :] = state.astype(BF16)
        pay[at, :] = run.astype(BF16)

    for k in range(blocks):
        at = pl.ds(k * BLOCK, BLOCK)
        if k:
            value_copy(k).wait()
            v[at, :] = jnp.transpose(dot(tok[...], w_value[:, at]).astype(BF16))
            states(k - 1)
        else:
            for i in range(STEPS):
                here = pl.ds(i * STRETCH, STRETCH)
                token_copy(i).wait()
                if i == 0:
                    state_copy.wait()
                sp[here, :] = dot(tok[here, :], w_state[...]).astype(BF16)
                if i == 0:
                    value_copy(0).wait()
                if i == 1:
                    value_copy(2).start()
                if i == 2:
                    value_copy(3).start()
                v[at, here] = jnp.transpose(dot(tok[here, :], w_value[:, at]).astype(BF16))
    states(blocks - 1)


def project(docs, decays, tokens, w_value, w_state):
    rows, depth = tokens.shape
    heads = decays.shape[0]
    width = w_value.shape[1]
    return call(
        project_kernel,
        "project",
        [SMEM, FAR, FAR, FAR, FAR],
        [
            ((rows, depth), BF16),
            ((rows, 2 * STATE), BF16),
            ((width, rows), BF16),
            ((3, width, STATE), BF16),
            ((width + 3 * heads, STATE), BF16),
        ],
        (docs, *(far(x) for x in (decays, tokens, w_value, w_state))),
        [
            pltpu.VMEM((depth, width), BF16),
            pltpu.VMEM((depth, 2 * STATE), BF16),
            pltpu.VMEM((heads, rows), F32),
            pltpu.VMEM((STEPS, heads, STATE), F32),
            pltpu.VMEM((width, rows), BF16),
            pltpu.VMEM((heads, rows), F32),
            pltpu.SemaphoreType.DMA((STEPS + width // BLOCK + 2,)),
        ],
        mib=16,
        flops=2 * rows * depth * (width + 2 * STATE),
        moved=2 * (rows * depth + depth * width),
    )


def joined(docs, last_first, last_second):
    return (docs[last_first] == docs[last_second]).astype(F32)


def half_rows(core, *factors):
    half = factors[0].shape[0] // 2
    return [jnp.where(core == 0, x[:half], x[half:]) for x in factors]


def near_kernel(docs, own, peer, pay, earlier):
    heads = earlier.shape[0]
    half = heads // 2
    ctx = lax.axis_index("ctx")
    core, pair = ctx & 1, ctx >> 1
    second = core == 1
    total_own, total_peer = load_total(own, heads * HEAD, heads), load_total(peer, heads * HEAD, heads)
    keep = joined(docs, pair * 2 * STEPS + STEPS - 1, pair * 2 * STEPS + 2 * STEPS - 1)
    factor = jnp.exp(jnp.where(second, total_own, total_peer)) * keep
    own_by, peer_by = half_rows(core, jnp.where(second, 1.0, factor), jnp.where(second, factor, 1.0))
    for h in range(half):
        at = pl.ds(pl.multiple_of(core * (half * HEAD) + h * HEAD, HEAD), HEAD)
        row = slice(h, h + 1)
        pay[pl.ds(h * HEAD, HEAD), :] = (
            own[at, :].astype(F32) * own_by[row] + peer[at, :].astype(F32) * peer_by[row]
        ).astype(BF16)
    store_total(pay, half * HEAD, total_own + total_peer)
    earlier[...] = jnp.where(second, total_peer, 0.0)


def middle_kernel(docs, own, one, two, three, before, after, pay, left, earlier):
    heads = before.shape[0]
    half = heads // 2
    top = half * HEAD
    ctx = lax.axis_index("ctx")
    core, chip = ctx & 1, ctx >> 1
    odd, high = (chip & 1) == 1, (chip & 2) == 2
    t_own, t_one, t_two, t_three = (load_total(x, top, heads) for x in (own, one, two, three))
    last = lambda at: (at + 1) * 2 * STEPS - 1
    base, mine, theirs = (chip >> 2) << 2, (chip >> 1) << 1, ((chip >> 1) ^ 1) << 1
    keep_mine = joined(docs, last(mine), last(mine + 1))
    keep_theirs = joined(docs, last(theirs), last(theirs + 1))
    keep_all = joined(docs, last(base + 1), last(base + 3))
    by_mine = jnp.exp(jnp.where(odd, t_own, t_one)) * keep_mine
    by_theirs = jnp.exp(jnp.where(odd, t_two, t_three)) * keep_theirs
    by_all = jnp.exp(jnp.where(high, t_own + t_one, t_two + t_three)) * keep_all
    own_by, one_by, two_by, three_by, mine_by, theirs_by = half_rows(
        core,
        jnp.where(odd, 1.0, by_mine),
        jnp.where(odd, by_mine, 1.0),
        jnp.where(odd, 1.0, by_theirs),
        jnp.where(odd, by_theirs, 1.0),
        jnp.where(high, 1.0, by_all),
        jnp.where(high, by_all, 1.0),
    )
    for h in range(half):
        at = pl.ds(h * HEAD, HEAD)
        row = slice(h, h + 1)
        here = own[at, :].astype(F32) * own_by[row] + one[at, :].astype(F32) * one_by[row]
        there = two[at, :].astype(F32) * two_by[row] + three[at, :].astype(F32) * three_by[row]
        left[at, :] = one[at, :]
        left[pl.ds(top + h * HEAD, HEAD), :] = there.astype(BF16)
        pay[at, :] = (here * mine_by[row] + there * theirs_by[row]).astype(BF16)
    store_total(pay, top, (t_own + t_one) + (t_two + t_three))
    second = before[...] + jnp.where(odd, t_one, 0.0)
    earlier[pl.ds(0, heads), :] = second
    earlier[pl.ds(heads, heads), :] = second + jnp.where(high, t_two + t_three, 0.0)


def far_kernel(docs, one, two, three, before, after, left, earlier):
    heads = earlier.shape[0]
    half = heads // 2
    top = half * HEAD
    ctx = lax.axis_index("ctx")
    row_of = ctx >> 3
    odd = (row_of & 1) == 1
    t_one, t_two, t_three = (load_total(x, top, heads) for x in (one, two, three))
    theirs = ((row_of >> 1) ^ 1) << 1
    last = lambda at: (at + 1) * 8 * STEPS - 1
    factor = jnp.exp(jnp.where(odd, t_two, t_three)) * joined(docs, last(theirs), last(theirs + 1))
    two_by, three_by = half_rows(ctx & 1, jnp.where(odd, 1.0, factor), jnp.where(odd, factor, 1.0))
    for h in range(half):
        at = pl.ds(h * HEAD, HEAD)
        row = slice(h, h + 1)
        left[at, :] = one[at, :]
        left[pl.ds(top + h * HEAD, HEAD), :] = (
            two[at, :].astype(F32) * two_by[row] + three[at, :].astype(F32) * three_by[row]
        ).astype(BF16)
    earlier[...] = before[pl.ds(heads, heads), :] + jnp.where(odd, t_one, 0.0)


def assemble(core, own, peer, full):
    half = own.shape[0] // 2
    for level in range(2):
        source = pl.ds(level * half, half)
        full[level, pl.ds(pl.multiple_of(core * half, half), half), :] = own[source, :]
        full[level, pl.ds(pl.multiple_of((1 - core) * half, half), half), :] = peer[source, :]


def gate_kernel(tok, w_level, gate_hbm, out_hbm, gates, weight, w_out, w_gate, sems):
    blocks = w_gate.shape[1] // BLOCK

    def gate_copy(k):
        at = pl.ds(pl.multiple_of(k * BLOCK, BLOCK), BLOCK)
        return pltpu.make_async_copy(gate_hbm.at[:, at], w_gate.at[:, at], sems.at[k])

    out_copy = pltpu.make_async_copy(out_hbm, w_out, sems.at[blocks])
    gate_copy(0).start()
    gate_copy(1).start()
    cols = w_level.shape[1]
    heads = cols // LEVELS
    to_row, from_col = iota((cols, cols), 0), iota((cols, cols), 1)
    pick = ((to_row % heads) * LEVELS + to_row // heads == from_col).astype(BF16)
    turned = dot_nt(pick, dot(tok[...], w_level[...]).astype(BF16))
    weight[...] = jnp.maximum(turned, 0.0) + jnp.log1p(jnp.exp(-jnp.abs(turned)))

    @pl.loop(0, blocks)
    def _(k):
        gate_copy(k).wait()

        @pl.when(k + 2 < blocks)
        def _():
            gate_copy(k + 2).start()

        @pl.when(k == 1)
        def _():
            out_copy.start()

        at = pl.ds(pl.multiple_of(k * BLOCK, BLOCK), BLOCK)
        gates[at, :] = jnp.transpose(dot(tok[...], w_gate[:, at]).astype(BF16))

    out_copy.wait()


def remote_term(docs, ctx, bit, stretch_doc, weight, here, gone, source, c_out):
    heads = weight.shape[0] // LEVELS
    base = (ctx >> (bit + 1)) << (bit + 1)
    last_left = docs[(base + (1 << bit)) * STEPS - 1]
    live = ((((ctx >> bit) & 1) == 1) & (last_left == stretch_doc)).astype(F32)
    rows = weight[pl.ds((bit + 3) * heads, heads), here] * live
    if gone is not None:
        rows = rows * twice(jnp.exp(gone))
    return dot_nt(source[pl.ds(0, heads * HEAD), :], c_out), rows


def intra_kernel(docs, skip, weight, decays, v, sp, local, r0, ho, scaled_weight):
    heads = decays.shape[0]
    ctx = lax.axis_index("ctx")
    first = ctx * STEPS
    causal = iota((128, 128), 0) <= iota((128, 128), 1)
    lower = (iota((STRETCH, STRETCH), 0) >= iota((STRETCH, STRETCH), 1)).astype(F32)
    begin = jnp.zeros((heads, STATE), F32)
    previous = begin
    for index in range(STEPS):
        here = pl.ds(index * STRETCH, STRETCH)
        now = decays[:, here]
        cum = running_sums(now)
        cum_col = lax.dot_general(lower, now, NT, precision=HIGHEST, preferred_element_type=F32)
        total = lanes(cum[:, STRETCH - 1 :])
        grown = jnp.exp(cum)
        from_device = jnp.exp(cum + twice(begin))
        for level in range(3, LEVELS):
            rows = pl.ds(level * heads, heads)
            scaled_weight[rows, here] = weight[rows, here] * from_device
        b_in, c_out = sp[here, :STATE], sp[here, STATE:]
        scores = dot_nt(b_in, c_out)
        terms = []
        if index & 1:
            keep = joined(docs, first + index - 1, first + index)
            terms.append((0 if index == 1 else 2, weight[pl.ds(heads, heads), here] * grown * keep))
        if index & 2:
            keep = joined(docs, first + 1, first + index)
            factor = grown * jnp.exp(twice(previous)) if index == 3 else grown
            terms.append((1, weight[pl.ds(2 * heads, heads), here] * factor * keep))
        crosses = [(dot_nt(local[slot], c_out), row) for slot, row in terms]
        stretch_doc = docs[first + index]
        crosses.append(remote_term(docs, ctx, 0, stretch_doc, scaled_weight, here, None, r0, c_out))
        own_weight = weight[pl.ds(0, heads), here]
        for h in range(heads):
            at = slice(h * HEAD, (h + 1) * HEAD)
            col = cum_col[:, h : h + 1]
            row = cum[h : h + 1, :]

            def block(s, t, masked):
                decay = jnp.exp(
                    jnp.broadcast_to(row[:, t * 128 : t * 128 + 128], (128, 128)) - col[s * 128 : s * 128 + 128, :]
                )
                if masked:
                    decay = jnp.where(causal, decay, 0.0)
                return (scores[s * 128 : s * 128 + 128, t * 128 : t * 128 + 128] * decay).astype(BF16)

            vh = v[pl.ds(h * HEAD, HEAD), here]
            left = dot(vh[:, :128], block(0, 0, True))
            right = dot(vh, jnp.concatenate([block(0, 1, False), block(1, 1, True)], axis=0))
            out = skip[h] * vh.astype(F32) + own_weight[h : h + 1, :] * jnp.concatenate([left, right], axis=1)
            for cross, factor in crosses:
                out = out + factor[h : h + 1, :] * cross[at]
            ho[pl.ds(h * HEAD, HEAD), here] = out
        begin = begin + total
        previous = total


def late_kernel(docs, sp, ho, weight, e1, e23, own, peer, out, full):
    heads = e1.shape[0]
    ctx = lax.axis_index("ctx")
    assemble(ctx & 1, own, peer, full)
    for index in range(STEPS):
        here = pl.ds(index * STRETCH, STRETCH)
        c_out = sp[here, STATE:]
        stretch_doc = docs[ctx * STEPS + index]
        terms = [
            remote_term(docs, ctx, bit, stretch_doc, weight, here, gone, full.at[bit - 1], c_out)
            for bit, gone in ((1, e1[...]), (2, e23[pl.ds(0, heads), :]))
        ]
        for h in range(heads):
            at = pl.ds(h * HEAD, HEAD)
            total = ho[at, here]
            for cross, rows in terms:
                total = total + rows[h : h + 1, :] * cross[h * HEAD : (h + 1) * HEAD]
            out[at, here] = total


def finish_kernel(
    start, count, docs, gain, w_out, sp, gates, ho, weight, e23, e4, *refs
):
    far_own, far_peer, plus, minus, keep, own, acc, normed, full = refs
    ctx, tp = lax.axis_index("ctx"), lax.axis_index("tp")
    heads = e4.shape[0]
    assemble(ctx & 1, far_own, far_peer, full)
    for j in range(count):
        here = pl.ds((start + j) * STRETCH, STRETCH)
        c_out = sp[here, STATE:]
        stretch_doc = docs[ctx * STEPS + start + j]
        terms = [
            remote_term(docs, ctx, bit, stretch_doc, weight, here, gone, full.at[bit - 3], c_out)
            for bit, gone in ((3, e23[pl.ds(heads, heads), :]), (4, e4[...]))
        ]
        for h in range(heads):
            at = pl.ds(h * HEAD, HEAD)
            total = ho[at, here]
            for cross, rows in terms:
                total = total + rows[h : h + 1, :] * cross[h * HEAD : (h + 1) * HEAD]
            g = gates[at, here].astype(F32)
            gated = total * (g / (1.0 + jnp.exp(-g)))
            power = jnp.sum(gated * gated, axis=0, keepdims=True) * (1.0 / HEAD)
            acc[at, :] = gated * lax.rsqrt(power + 1e-5)
        normed[pl.ds(j * STRETCH, STRETCH), :] = (jnp.transpose(acc[...]) * gain[...]).astype(BF16)
    quarter = w_out.shape[1] // 8

    def piece(shift, side):
        col = pl.multiple_of((((tp + shift) & 3) * 2 + side) * quarter, quarter)
        return dot(normed[...], w_out[:, pl.ds(col, quarter)]).astype(BF16)

    first, second = pl.ds(0, quarter), pl.ds(quarter, quarter)
    plus[:, first] = piece(2, 0)
    plus[:, second] = piece(1, 1)
    minus[:, first] = piece(2, 1)
    minus[:, second] = piece(3, 0)
    keep[:, first] = piece(1, 0)
    keep[:, second] = piece(3, 1)
    own[:, first] = piece(0, 0)
    own[:, second] = piece(0, 1)


def finish(start, stop, docs, gain, w_out, *operands):
    count = stop - start
    width, depth = w_out.shape
    rows = count * STRETCH
    return call(
        functools.partial(finish_kernel, start, count),
        f"finish{start}",
        [SMEM] + [VMEM] * (2 + len(operands)),
        [((rows, depth // 4), BF16)] * 4,
        (docs, gain, w_out, *operands),
        [
            pltpu.VMEM((width, STRETCH), F32),
            pltpu.VMEM((rows, width), BF16),
            pltpu.VMEM((2, width, STATE), BF16),
        ],
        mib=16,
        flops=4 * rows * depth * width,
        moved=2 * width * depth + 8 * rows * width,
    )


def per_device(tokens, w_value, w_gate, w_state, w_level, log_decay, skip_weight, norm_gain, doc_ids, w_out):
    rows, depth = tokens.shape
    width = w_value.shape[1]
    heads = log_decay.shape[1]
    docs = far(doc_ids)
    decays = jnp.transpose(log_decay)
    part = ((width // 2 + 3 * heads, STATE), BF16)
    tail = ((width, STATE), BF16)
    gone = ((heads, STATE), F32)

    def across(x, by):
        return lax.ppermute(x, "ctx", [(i, i ^ by) for i in range(32)])

    def turn(x, by):
        return lax.ppermute(x, "tp", [(i, (i + by) % 4) for i in range(4)])

    tok, sp, v, local, pay0 = project(docs, decays, tokens, w_value, w_state)
    peer = across(pay0, 1)
    pay1, e1 = call(
        near_kernel, "near", [SMEM] + [VMEM] * 2, [part, gone], (docs, pay0, peer)
    )
    ys = [across(pay1, by) for by in (4, 2, 6)]
    gates, weight, w_out_near = call(
        gate_kernel,
        "gate",
        [VMEM] * 2 + [FAR] * 2,
        [((width, rows), BF16), ((heads * LEVELS, rows), F32), (w_out.shape, BF16)],
        (tok, w_level, far(w_gate), far(w_out)),
        [pltpu.VMEM(w_gate.shape, BF16), pltpu.SemaphoreType.DMA((width // BLOCK + 1,))],
        mib=16,
        flops=2 * rows * depth * (width + STATE),
        moved=2 * (rows * depth + depth * width),
    )
    y2, y1, y3 = ys
    pay2, mid_own, e23 = call(
        middle_kernel,
        "middle",
        [SMEM] + [VMEM] * 6,
        [part, tail, ((2 * heads, STATE), F32)],
        (docs, pay1, y1, y2, y3, e1, weight),
    )
    x2, x1, x3 = (across(pay2, by) for by in (16, 8, 24))
    mid_peer = across(mid_own, 1)
    ho, scaled_weight = call(
        intra_kernel,
        "intra",
        [SMEM] * 2 + [VMEM] * 6,
        [((width, rows), F32), ((heads * LEVELS, rows), F32)],
        (docs, skip_weight, weight, decays, v, sp, local, peer),
        mib=12,
        flops=6 << 30,
        moved=8 << 20,
    )
    far_own, e4 = call(
        far_kernel,
        "far",
        [SMEM] + [VMEM] * 5,
        [tail, gone],
        (docs, x1, x2, x3, e23, scaled_weight),
    )
    far_peer = across(far_own, 1)
    (ho,) = call(
        late_kernel,
        "late",
        [SMEM] + [VMEM] * 7,
        [((width, rows), F32)],
        (docs, sp, ho, scaled_weight, e1, e23, mid_own, mid_peer),
        [pltpu.VMEM((2, width, STATE), BF16)],
        mib=8,
        flops=2 << 30,
        moved=4 << 20,
    )
    gain = norm_gain.reshape(1, -1)
    results = []
    half = w_out.shape[1] // 8
    for lo, hi in CHUNKS:
        plus, minus, keep, own = finish(
            lo, hi, docs, gain, w_out_near, sp, gates, ho, scaled_weight, e23, e4, far_own, far_peer
        )
        from_below, from_above = turn(plus, 1), turn(minus, 3)
        on_plus = (keep[:, :half].astype(F32) + from_below[:, :half].astype(F32)).astype(BF16)
        on_minus = (keep[:, half:].astype(F32) + from_above[:, :half].astype(F32)).astype(BF16)
        last_below, last_above = turn(on_plus, 1), turn(on_minus, 3)
        first = own[:, :half].astype(F32) + from_above[:, half:].astype(F32) + last_below.astype(F32)
        second = own[:, half:].astype(F32) + from_below[:, half:].astype(F32) + last_above.astype(F32)
        results.append(jnp.concatenate([first, second], axis=1).astype(BF16))
    return jnp.concatenate(results, axis=0)


def solution(mesh):
    placed = (
        P("ctx", None),
        P(None, "tp"),
        P(None, "tp"),
        P(),
        P(None, "tp"),
        P("ctx", "tp"),
        P("tp"),
        P("tp"),
        P(),
        P("tp", None),
    )
    return jax.shard_map(per_device, mesh=mesh, in_specs=placed, out_specs=P("ctx", "tp"), check_vma=False)
```

```python
import functools

import jax
import jax.numpy as jnp
from jax import lax
from jax.experimental import pallas as pl
from jax.experimental.pallas import tpu as pltpu
from jax.sharding import PartitionSpec as P

STRETCH = 256
STEPS = 4
HEAD = 64
STATE = 128
LEVELS = 8
BLOCK = 256
GATE_BLOCK = 512
F32 = jnp.float32
BF16 = jnp.bfloat16
NT = (((1,), (1,)), ((), ()))
CHUNKS = ((0, 2), (2, 4))
SMEM = pl.BlockSpec(memory_space=pltpu.SMEM)
VMEM = pl.BlockSpec(memory_space=pltpu.VMEM)
FAR = pl.BlockSpec(memory_space=pltpu.HBM)


def dot(a, b):
    return jnp.dot(a, b, preferred_element_type=F32)


def dot_nt(a, b):
    return lax.dot_general(a, b, NT, preferred_element_type=F32)


def iota(shape, dim):
    return lax.broadcasted_iota(jnp.int32, shape, dim)


def far(x):
    return pltpu.with_memory_space_constraint(x, pltpu.HBM)


def twice(x):
    return jnp.concatenate([x, x], axis=1)


def split(x):
    high = x.astype(BF16)
    rest = x - high.astype(F32)
    middle = rest.astype(BF16)
    low = (rest - middle.astype(F32)).astype(BF16)
    return jnp.concatenate([high, middle, low], axis=0)


def running_sums(decays):
    rows = decays.shape[0]
    shape = (STRETCH, STRETCH)
    parts = dot(split(decays), (iota(shape, 0) <= iota(shape, 1)).astype(BF16))
    return (parts[:rows] + parts[rows : 2 * rows]) + parts[2 * rows :]


def lanes(column):
    return jnp.broadcast_to(column, (column.shape[0], STATE))


def store_total(ref, top, total):
    heads = total.shape[0]
    high = total.astype(BF16)
    rest = total - high.astype(F32)
    middle = rest.astype(BF16)
    low = (rest - middle.astype(F32)).astype(BF16)
    ref[pl.ds(top, heads), :] = high
    ref[pl.ds(top + heads, heads), :] = middle
    ref[pl.ds(top + 2 * heads, heads), :] = low


def load_total(ref, top, heads):
    parts = [ref[pl.ds(top + k * heads, heads), :].astype(F32) for k in range(3)]
    return (parts[0] + parts[1]) + parts[2]


def call(kernel, name, in_specs, out_shape, args, scratch=(), mib=8, flops=1 << 20, moved=1 << 20, out_specs=None):
    return pl.pallas_call(
        kernel,
        name=name,
        in_specs=in_specs,
        out_specs=[VMEM] * len(out_shape),
        out_shape=[jax.ShapeDtypeStruct(*x) for x in out_shape],
        scratch_shapes=list(scratch),
        compiler_params=pltpu.CompilerParams(vmem_limit_bytes=mib << 20),
        cost_estimate=pl.CostEstimate(flops=flops, bytes_accessed=moved, transcendentals=0),
    )(*args)


def project_kernel(
    docs, decays_hbm, tok_hbm, value_hbm, state_hbm, tok, sp, v, local, pay, w_value, w_state, tail, grow, scaled, decays,
    sems,
):
    heads = decays.shape[0]
    blocks = w_value.shape[1] // BLOCK
    per_block = BLOCK // HEAD

    def token_copy(i):
        at = pl.ds(i * STRETCH, STRETCH)
        return pltpu.make_async_copy(tok_hbm.at[at, :], tok.at[at, :], sems.at[i])

    def value_copy(k):
        at = pl.ds(k * BLOCK, BLOCK)
        return pltpu.make_async_copy(value_hbm.at[:, at], w_value.at[:, at], sems.at[STEPS + k])

    state_copy = pltpu.make_async_copy(state_hbm, w_state, sems.at[STEPS + blocks])
    decay_copy = pltpu.make_async_copy(decays_hbm, decays, sems.at[STEPS + blocks + 1])
    decay_copy.start()
    token_copy(0).start()
    state_copy.start()
    value_copy(0).start()
    for i in range(1, STEPS):
        token_copy(i).start()
    value_copy(1).start()

    decay_copy.wait()
    stacked = jnp.concatenate([decays[:, pl.ds(i * STRETCH, STRETCH)] for i in range(STEPS)], axis=0)
    cum = running_sums(stacked)
    total = lanes(cum[:, STRETCH - 1 :])
    rest = jnp.exp(twice(total) - cum)
    first = lax.axis_index("ctx") * STEPS
    whole = jnp.zeros((heads, STATE), F32)
    for i in range(STEPS):
        rows = slice(i * heads, (i + 1) * heads)
        tail[:, pl.ds(i * STRETCH, STRETCH)] = rest[rows]
        same = (docs[first + max(i - 1, 0)] == docs[first + i]).astype(F32)
        grow[i] = jnp.exp(total[rows]) * same
        whole = whole + total[rows]
    store_total(pay, heads * HEAD, whole)

    def states(k):
        at = pl.ds(k * BLOCK, BLOCK)
        for h in range(per_block):
            rows = pl.ds(k * BLOCK + h * HEAD, HEAD)
            row = k * per_block + h
            scaled[rows, :] = (v[rows, :].astype(F32) * tail[row : row + 1, :]).astype(BF16)
        run = None
        for i in range(STEPS):
            here = pl.ds(i * STRETCH, STRETCH)
            state = dot(scaled[at, here], sp[here, :STATE])
            if i == 0:
                run = state
                local[0, at, :] = state.astype(BF16)
                continue
            factor = jnp.concatenate(
                [
                    jnp.broadcast_to(grow[i, k * per_block + h : k * per_block + h + 1, :], (HEAD, STATE))
                    for h in range(per_block)
                ],
                axis=0,
            )
            run = run * factor + state
            if i == 1:
                local[1, at, :] = run.astype(BF16)
            if i == 2:
                local[2, at, :] = state.astype(BF16)
        pay[at, :] = run.astype(BF16)

    for k in range(blocks):
        at = pl.ds(k * BLOCK, BLOCK)
        if k:
            value_copy(k).wait()
            for i in range(STEPS):
                here = pl.ds(i * STRETCH, STRETCH)
                v[at, here] = jnp.transpose(dot(tok[here, :], w_value[:, at]).astype(BF16))
            states(k - 1)
        else:
            for i in range(STEPS):
                here = pl.ds(i * STRETCH, STRETCH)
                token_copy(i).wait()
                if i == 0:
                    state_copy.wait()
                sp[here, :] = dot(tok[here, :], w_state[...]).astype(BF16)
                if i == 0:
                    value_copy(0).wait()
                if i == 1:
                    value_copy(2).start()
                if i == 2:
                    value_copy(3).start()
                v[at, here] = jnp.transpose(dot(tok[here, :], w_value[:, at]).astype(BF16))
    states(blocks - 1)


def project(docs, decays, tokens, w_value, w_state):
    rows, depth = tokens.shape
    heads = decays.shape[0]
    width = w_value.shape[1]
    return call(
        project_kernel,
        "project",
        [SMEM, FAR, FAR, FAR, FAR],
        [
            ((rows, depth), BF16),
            ((rows, 2 * STATE), BF16),
            ((width, rows), BF16),
            ((3, width, STATE), BF16),
            ((width + 3 * heads, STATE), BF16),
        ],
        (docs, *(far(x) for x in (decays, tokens, w_value, w_state))),
        [
            pltpu.VMEM((depth, width), BF16),
            pltpu.VMEM((depth, 2 * STATE), BF16),
            pltpu.VMEM((heads, rows), F32),
            pltpu.VMEM((STEPS, heads, STATE), F32),
            pltpu.VMEM((width, rows), BF16),
            pltpu.VMEM((heads, rows), F32),
            pltpu.SemaphoreType.DMA((STEPS + width // BLOCK + 2,)),
        ],
        mib=16,
        flops=2 * rows * depth * (width + 2 * STATE),
        moved=2 * (rows * depth + depth * width),
    )


def joined(docs, last_first, last_second):
    return (docs[last_first] == docs[last_second]).astype(F32)


def half_rows(core, *factors):
    half = factors[0].shape[0] // 2
    return [jnp.where(core == 0, x[:half], x[half:]) for x in factors]


def near_kernel(docs, own, peer, pay, earlier):
    heads = earlier.shape[0]
    half = heads // 2
    ctx = lax.axis_index("ctx")
    core, pair = ctx & 1, ctx >> 1
    second = core == 1
    total_own, total_peer = load_total(own, heads * HEAD, heads), load_total(peer, heads * HEAD, heads)
    keep = joined(docs, pair * 2 * STEPS + STEPS - 1, pair * 2 * STEPS + 2 * STEPS - 1)
    factor = jnp.exp(jnp.where(second, total_own, total_peer)) * keep
    own_by, peer_by = half_rows(core, jnp.where(second, 1.0, factor), jnp.where(second, factor, 1.0))
    for h in range(half):
        at = pl.ds(pl.multiple_of(core * (half * HEAD) + h * HEAD, HEAD), HEAD)
        row = slice(h, h + 1)
        pay[pl.ds(h * HEAD, HEAD), :] = (
            own[at, :].astype(F32) * own_by[row] + peer[at, :].astype(F32) * peer_by[row]
        ).astype(BF16)
    store_total(pay, half * HEAD, total_own + total_peer)
    earlier[...] = jnp.where(second, total_peer, 0.0)


def middle_kernel(docs, own, one, two, three, before, after, pay, left, earlier):
    heads = before.shape[0]
    half = heads // 2
    top = half * HEAD
    ctx = lax.axis_index("ctx")
    core, chip = ctx & 1, ctx >> 1
    odd, high = (chip & 1) == 1, (chip & 2) == 2
    t_own, t_one, t_two, t_three = (load_total(x, top, heads) for x in (own, one, two, three))
    last = lambda at: (at + 1) * 2 * STEPS - 1
    base, mine, theirs = (chip >> 2) << 2, (chip >> 1) << 1, ((chip >> 1) ^ 1) << 1
    keep_mine = joined(docs, last(mine), last(mine + 1))
    keep_theirs = joined(docs, last(theirs), last(theirs + 1))
    keep_all = joined(docs, last(base + 1), last(base + 3))
    by_mine = jnp.exp(jnp.where(odd, t_own, t_one)) * keep_mine
    by_theirs = jnp.exp(jnp.where(odd, t_two, t_three)) * keep_theirs
    by_all = jnp.exp(jnp.where(high, t_own + t_one, t_two + t_three)) * keep_all
    own_by, one_by, two_by, three_by, mine_by, theirs_by = half_rows(
        core,
        jnp.where(odd, 1.0, by_mine),
        jnp.where(odd, by_mine, 1.0),
        jnp.where(odd, 1.0, by_theirs),
        jnp.where(odd, by_theirs, 1.0),
        jnp.where(high, 1.0, by_all),
        jnp.where(high, by_all, 1.0),
    )
    for h in range(half):
        at = pl.ds(h * HEAD, HEAD)
        row = slice(h, h + 1)
        here = own[at, :].astype(F32) * own_by[row] + one[at, :].astype(F32) * one_by[row]
        there = two[at, :].astype(F32) * two_by[row] + three[at, :].astype(F32) * three_by[row]
        left[at, :] = one[at, :]
        left[pl.ds(top + h * HEAD, HEAD), :] = there.astype(BF16)
        pay[at, :] = (here * mine_by[row] + there * theirs_by[row]).astype(BF16)
    store_total(pay, top, (t_own + t_one) + (t_two + t_three))
    second = before[...] + jnp.where(odd, t_one, 0.0)
    earlier[pl.ds(0, heads), :] = second
    earlier[pl.ds(heads, heads), :] = second + jnp.where(high, t_two + t_three, 0.0)


def far_kernel(docs, one, two, three, before, after, left, earlier):
    heads = earlier.shape[0]
    half = heads // 2
    top = half * HEAD
    ctx = lax.axis_index("ctx")
    row_of = ctx >> 3
    odd = (row_of & 1) == 1
    t_one, t_two, t_three = (load_total(x, top, heads) for x in (one, two, three))
    theirs = ((row_of >> 1) ^ 1) << 1
    last = lambda at: (at + 1) * 8 * STEPS - 1
    factor = jnp.exp(jnp.where(odd, t_two, t_three)) * joined(docs, last(theirs), last(theirs + 1))
    two_by, three_by = half_rows(ctx & 1, jnp.where(odd, 1.0, factor), jnp.where(odd, factor, 1.0))
    for h in range(half):
        at = pl.ds(h * HEAD, HEAD)
        row = slice(h, h + 1)
        left[at, :] = one[at, :]
        left[pl.ds(top + h * HEAD, HEAD), :] = (
            two[at, :].astype(F32) * two_by[row] + three[at, :].astype(F32) * three_by[row]
        ).astype(BF16)
    earlier[...] = before[pl.ds(heads, heads), :] + jnp.where(odd, t_one, 0.0)


def assemble(core, own, peer, full):
    half = own.shape[0] // 2
    for level in range(2):
        source = pl.ds(level * half, half)
        full[level, pl.ds(pl.multiple_of(core * half, half), half), :] = own[source, :]
        full[level, pl.ds(pl.multiple_of((1 - core) * half, half), half), :] = peer[source, :]


SEND_ORDER = ((2, 0), (1, 1), (2, 1), (3, 0), (1, 0), (3, 1), (0, 0), (0, 1))


def gate_kernel(tok, w_level, gate_hbm, out_hbm, gates, weight, w_out, w_gate, sems):
    blocks = w_gate.shape[1] // GATE_BLOCK
    tp = lax.axis_index("tp")
    eighth = w_out.shape[1] // len(SEND_ORDER)

    def gate_copy(k):
        at = pl.ds(k * GATE_BLOCK, GATE_BLOCK)
        return pltpu.make_async_copy(gate_hbm.at[:, at], w_gate.at[:, at], sems.at[k])

    def out_copy(j):
        shift, side = SEND_ORDER[j]
        source = pl.ds(pl.multiple_of((((tp + shift) & 3) * 2 + side) * eighth, eighth), eighth)
        return pltpu.make_async_copy(out_hbm.at[:, source], w_out.at[:, pl.ds(j * eighth, eighth)], sems.at[blocks + j])

    for k in range(blocks):
        gate_copy(k).start()
    cols = w_level.shape[1]
    heads = cols // LEVELS
    to_row, from_col = iota((cols, cols), 0), iota((cols, cols), 1)
    pick = ((to_row % heads) * LEVELS + to_row // heads == from_col).astype(BF16)
    turned = dot_nt(pick, dot(tok[...], w_level[...]).astype(BF16))
    weight[...] = jnp.maximum(turned, 0.0) + jnp.log1p(jnp.exp(-jnp.abs(turned)))
    for k in range(blocks):
        gate_copy(k).wait()
        if k == 0:
            for j in range(len(SEND_ORDER)):
                out_copy(j).start()
        at = pl.ds(k * GATE_BLOCK, GATE_BLOCK)
        gates[at, :] = jnp.transpose(dot(tok[...], w_gate[:, at]).astype(BF16))
    for j in range(len(SEND_ORDER)):
        out_copy(j).wait()


def remote_term(docs, ctx, bit, stretch_doc, weight, here, gone, source, c_out):
    heads = weight.shape[0] // LEVELS
    base = (ctx >> (bit + 1)) << (bit + 1)
    last_left = docs[(base + (1 << bit)) * STEPS - 1]
    live = ((((ctx >> bit) & 1) == 1) & (last_left == stretch_doc)).astype(F32)
    rows = weight[pl.ds((bit + 3) * heads, heads), here] * live
    if gone is not None:
        rows = rows * twice(jnp.exp(gone))
    return dot_nt(source[pl.ds(0, heads * HEAD), :], c_out), rows


def intra_kernel(docs, skip, weight, decays, v, sp, local, r0, ho, scaled_weight):
    heads = decays.shape[0]
    ctx = lax.axis_index("ctx")
    first = ctx * STEPS
    causal = iota((128, 128), 0) <= iota((128, 128), 1)
    lower = (iota((STRETCH, STRETCH), 0) >= iota((STRETCH, STRETCH), 1)).astype(BF16)
    begin = jnp.zeros((heads, STATE), F32)
    previous = begin
    for index in range(STEPS):
        here = pl.ds(index * STRETCH, STRETCH)
        now = decays[:, here]
        cum = running_sums(now)
        parts = dot_nt(lower, split(now))
        cum_col = (parts[:, :heads] + parts[:, heads : 2 * heads]) + parts[:, 2 * heads :]
        total = lanes(cum[:, STRETCH - 1 :])
        grown = jnp.exp(cum)
        from_device = jnp.exp(cum + twice(begin))
        for level in range(3, LEVELS):
            rows = pl.ds(level * heads, heads)
            scaled_weight[rows, here] = weight[rows, here] * from_device
        b_in, c_out = sp[here, :STATE], sp[here, STATE:]
        scores = dot_nt(b_in, c_out)
        terms = []
        if index & 1:
            keep = joined(docs, first + index - 1, first + index)
            terms.append((0 if index == 1 else 2, weight[pl.ds(heads, heads), here] * grown * keep))
        if index & 2:
            keep = joined(docs, first + 1, first + index)
            factor = grown * jnp.exp(twice(previous)) if index == 3 else grown
            terms.append((1, weight[pl.ds(2 * heads, heads), here] * factor * keep))
        crosses = [(dot_nt(local[slot], c_out), row) for slot, row in terms]
        stretch_doc = docs[first + index]
        crosses.append(remote_term(docs, ctx, 0, stretch_doc, scaled_weight, here, None, r0, c_out))
        own_weight = weight[pl.ds(0, heads), here]
        for h in range(heads):
            at = slice(h * HEAD, (h + 1) * HEAD)
            col = cum_col[:, h : h + 1]
            row = cum[h : h + 1, :]

            def block(s, t, masked):
                decay = jnp.exp(
                    jnp.broadcast_to(row[:, t * 128 : t * 128 + 128], (128, 128)) - col[s * 128 : s * 128 + 128, :]
                )
                if masked:
                    decay = jnp.where(causal, decay, 0.0)
                return (scores[s * 128 : s * 128 + 128, t * 128 : t * 128 + 128] * decay).astype(BF16)

            vh = v[pl.ds(h * HEAD, HEAD), here]
            left = dot(vh[:, :128], block(0, 0, True))
            right = dot(vh, jnp.concatenate([block(0, 1, False), block(1, 1, True)], axis=0))
            out = skip[h] * vh.astype(F32) + own_weight[h : h + 1, :] * jnp.concatenate([left, right], axis=1)
            for cross, factor in crosses:
                out = out + factor[h : h + 1, :] * cross[at]
            ho[pl.ds(h * HEAD, HEAD), here] = out
        begin = begin + total
        previous = total


def late_kernel(docs, sp, ho, weight, e1, e23, own, peer, out, full):
    heads = e1.shape[0]
    ctx = lax.axis_index("ctx")
    assemble(ctx & 1, own, peer, full)
    for index in range(STEPS):
        here = pl.ds(index * STRETCH, STRETCH)
        c_out = sp[here, STATE:]
        stretch_doc = docs[ctx * STEPS + index]
        terms = [
            remote_term(docs, ctx, bit, stretch_doc, weight, here, gone, full.at[bit - 1], c_out)
            for bit, gone in ((1, e1[...]), (2, e23[pl.ds(0, heads), :]))
        ]
        for h in range(heads):
            at = pl.ds(h * HEAD, HEAD)
            total = ho[at, here]
            for cross, rows in terms:
                total = total + rows[h : h + 1, :] * cross[h * HEAD : (h + 1) * HEAD]
            out[at, here] = total


def finish_kernel(
    start, count, docs, gain, w_out, sp, gates, ho, weight, e23, e4, *refs
):
    far_own, far_peer, plus, minus, keep, own, acc, normed, full = refs
    ctx = lax.axis_index("ctx")
    heads = e4.shape[0]
    assemble(ctx & 1, far_own, far_peer, full)
    for j in range(count):
        here = pl.ds((start + j) * STRETCH, STRETCH)
        c_out = sp[here, STATE:]
        stretch_doc = docs[ctx * STEPS + start + j]
        terms = [
            remote_term(docs, ctx, bit, stretch_doc, weight, here, gone, full.at[bit - 3], c_out)
            for bit, gone in ((3, e23[pl.ds(heads, heads), :]), (4, e4[...]))
        ]
        for h in range(heads):
            at = pl.ds(h * HEAD, HEAD)
            total = ho[at, here]
            for cross, rows in terms:
                total = total + rows[h : h + 1, :] * cross[h * HEAD : (h + 1) * HEAD]
            g = gates[at, here].astype(F32)
            gated = total * (g / (1.0 + jnp.exp(-g)))
            power = jnp.sum(gated * gated, axis=0, keepdims=True) * (1.0 / HEAD)
            acc[at, :] = gated * lax.rsqrt(power + 1e-5)
        normed[pl.ds(j * STRETCH, STRETCH), :] = (jnp.transpose(acc[...]) * gain[...]).astype(BF16)
    quarter = w_out.shape[1] // 4
    for j, out in enumerate((plus, minus, keep, own)):
        out[...] = dot(normed[...], w_out[:, pl.ds(j * quarter, quarter)]).astype(BF16)


def finish(start, stop, docs, gain, w_out, *operands):
    count = stop - start
    width, depth = w_out.shape
    rows = count * STRETCH
    return call(
        functools.partial(finish_kernel, start, count),
        f"finish{start}",
        [SMEM] + [VMEM] * (2 + len(operands)),
        [((rows, depth // 4), BF16)] * 4,
        (docs, gain, w_out, *operands),
        [
            pltpu.VMEM((width, STRETCH), F32),
            pltpu.VMEM((rows, width), BF16),
            pltpu.VMEM((2, width, STATE), BF16),
        ],
        mib=16,
        flops=4 * rows * depth * width,
        moved=2 * width * depth + 8 * rows * width,
    )


def per_device(tokens, w_value, w_gate, w_state, w_level, log_decay, skip_weight, norm_gain, doc_ids, w_out):
    rows, depth = tokens.shape
    width = w_value.shape[1]
    heads = log_decay.shape[1]
    docs = far(doc_ids)
    decays = jnp.transpose(log_decay)
    part = ((width // 2 + 3 * heads, STATE), BF16)
    tail = ((width, STATE), BF16)
    gone = ((heads, STATE), F32)

    def across(x, by):
        return lax.ppermute(x, "ctx", [(i, i ^ by) for i in range(32)])

    def turn(x, by):
        return lax.ppermute(x, "tp", [(i, (i + by) % 4) for i in range(4)])

    tok, sp, v, local, pay0 = project(docs, decays, tokens, w_value, w_state)
    peer = across(pay0, 1)
    pay1, e1 = call(
        near_kernel, "near", [SMEM] + [VMEM] * 2, [part, gone], (docs, pay0, peer)
    )
    ys = [across(pay1, by) for by in (4, 2, 6)]
    gates, weight, w_out_near = call(
        gate_kernel,
        "gate",
        [VMEM] * 2 + [FAR] * 2,
        [((width, rows), BF16), ((heads * LEVELS, rows), F32), (w_out.shape, BF16)],
        (tok, w_level, far(w_gate), far(w_out)),
        [pltpu.VMEM(w_gate.shape, BF16), pltpu.SemaphoreType.DMA((width // GATE_BLOCK + len(SEND_ORDER),))],
        mib=16,
        flops=2 * rows * depth * (width + STATE),
        moved=2 * (rows * depth + depth * width),
    )
    y2, y1, y3 = ys
    pay2, mid_own, e23 = call(
        middle_kernel,
        "middle",
        [SMEM] + [VMEM] * 6,
        [part, tail, ((2 * heads, STATE), F32)],
        (docs, pay1, y1, y2, y3, e1, weight),
    )
    x2, x1, x3 = (across(pay2, by) for by in (16, 8, 24))
    mid_peer = across(mid_own, 1)
    ho, scaled_weight = call(
        intra_kernel,
        "intra",
        [SMEM] * 2 + [VMEM] * 6,
        [((width, rows), F32), ((heads * LEVELS, rows), F32)],
        (docs, skip_weight, weight, decays, v, sp, local, peer),
        mib=12,
        flops=6 << 30,
        moved=8 << 20,
    )
    far_own, e4 = call(
        far_kernel,
        "far",
        [SMEM] + [VMEM] * 5,
        [tail, gone],
        (docs, x1, x2, x3, e23, scaled_weight),
    )
    far_peer = across(far_own, 1)
    (ho,) = call(
        late_kernel,
        "late",
        [SMEM] + [VMEM] * 7,
        [((width, rows), F32)],
        (docs, sp, ho, scaled_weight, e1, e23, mid_own, mid_peer),
        [pltpu.VMEM((2, width, STATE), BF16)],
        mib=8,
        flops=2 << 30,
        moved=4 << 20,
    )
    gain = norm_gain.reshape(1, -1)
    results = []
    half = w_out.shape[1] // 8
    for lo, hi in CHUNKS:
        plus, minus, keep, own = finish(
            lo, hi, docs, gain, w_out_near, sp, gates, ho, scaled_weight, e23, e4, far_own, far_peer
        )
        from_below, from_above = turn(plus, 1), turn(minus, 3)
        on_plus = (keep[:, :half].astype(F32) + from_below[:, :half].astype(F32)).astype(BF16)
        on_minus = (keep[:, half:].astype(F32) + from_above[:, :half].astype(F32)).astype(BF16)
        last_below, last_above = turn(on_plus, 1), turn(on_minus, 3)
        first = own[:, :half].astype(F32) + from_above[:, half:].astype(F32) + last_below.astype(F32)
        second = own[:, half:].astype(F32) + from_below[:, half:].astype(F32) + last_above.astype(F32)
        results.append(jnp.concatenate([first, second], axis=1).astype(BF16))
    return jnp.concatenate(results, axis=0)


def solution(mesh):
    placed = (
        P("ctx", None),
        P(None, "tp"),
        P(None, "tp"),
        P(),
        P(None, "tp"),
        P("ctx", "tp"),
        P("tp"),
        P("tp"),
        P(),
        P("tp", None),
    )
    return jax.shard_map(per_device, mesh=mesh, in_specs=placed, out_specs=P("ctx", "tp"), check_vma=False)
```

```python
import functools

import jax
import jax.numpy as jnp
from jax import lax
from jax.experimental import pallas as pl
from jax.experimental.pallas import tpu as pltpu
from jax.sharding import PartitionSpec as P

STRETCH = 256
STEPS = 4
HEAD = 64
STATE = 128
LEVELS = 8
BLOCK = 256
GATE_BLOCK = 512
F32 = jnp.float32
BF16 = jnp.bfloat16
NT = (((1,), (1,)), ((), ()))
CHUNKS = ((0, 2), (2, 3), (3, 4))
SMEM = pl.BlockSpec(memory_space=pltpu.SMEM)
VMEM = pl.BlockSpec(memory_space=pltpu.VMEM)
FAR = pl.BlockSpec(memory_space=pltpu.HBM)


def dot(a, b):
    return jnp.dot(a, b, preferred_element_type=F32)


def dot_nt(a, b):
    return lax.dot_general(a, b, NT, preferred_element_type=F32)


def iota(shape, dim):
    return lax.broadcasted_iota(jnp.int32, shape, dim)


def far(x):
    return pltpu.with_memory_space_constraint(x, pltpu.HBM)


def twice(x):
    return jnp.concatenate([x, x], axis=1)


def split(x):
    high = x.astype(BF16)
    rest = x - high.astype(F32)
    middle = rest.astype(BF16)
    low = (rest - middle.astype(F32)).astype(BF16)
    return jnp.concatenate([high, middle, low], axis=0)


def running_sums(decays):
    rows = decays.shape[0]
    shape = (STRETCH, STRETCH)
    parts = dot(split(decays), (iota(shape, 0) <= iota(shape, 1)).astype(BF16))
    return (parts[:rows] + parts[rows : 2 * rows]) + parts[2 * rows :]


def lanes(column):
    return jnp.broadcast_to(column, (column.shape[0], STATE))


def store_total(ref, top, total):
    heads = total.shape[0]
    high = total.astype(BF16)
    rest = total - high.astype(F32)
    middle = rest.astype(BF16)
    low = (rest - middle.astype(F32)).astype(BF16)
    ref[pl.ds(top, heads), :] = high
    ref[pl.ds(top + heads, heads), :] = middle
    ref[pl.ds(top + 2 * heads, heads), :] = low


def load_total(ref, top, heads):
    parts = [ref[pl.ds(top + k * heads, heads), :].astype(F32) for k in range(3)]
    return (parts[0] + parts[1]) + parts[2]


def call(kernel, name, in_specs, out_shape, args, scratch=(), mib=8, flops=1 << 20, moved=1 << 20, out_specs=None):
    return pl.pallas_call(
        kernel,
        name=name,
        in_specs=in_specs,
        out_specs=[VMEM] * len(out_shape),
        out_shape=[jax.ShapeDtypeStruct(*x) for x in out_shape],
        scratch_shapes=list(scratch),
        compiler_params=pltpu.CompilerParams(vmem_limit_bytes=mib << 20),
        cost_estimate=pl.CostEstimate(flops=flops, bytes_accessed=moved, transcendentals=0),
    )(*args)


def project_kernel(
    docs, decays_hbm, tok_hbm, value_hbm, state_hbm, tok, sp, v, local, pay, w_value, w_state, tail, grow, scaled, decays,
    sems,
):
    heads = decays.shape[0]
    blocks = w_value.shape[1] // BLOCK
    per_block = BLOCK // HEAD

    def token_copy(i):
        at = pl.ds(i * STRETCH, STRETCH)
        return pltpu.make_async_copy(tok_hbm.at[at, :], tok.at[at, :], sems.at[i])

    def value_copy(k):
        at = pl.ds(k * BLOCK, BLOCK)
        return pltpu.make_async_copy(value_hbm.at[:, at], w_value.at[:, at], sems.at[STEPS + k])

    state_copy = pltpu.make_async_copy(state_hbm, w_state, sems.at[STEPS + blocks])
    decay_copy = pltpu.make_async_copy(decays_hbm, decays, sems.at[STEPS + blocks + 1])
    decay_copy.start()
    token_copy(0).start()
    state_copy.start()
    value_copy(0).start()
    for i in range(1, STEPS):
        token_copy(i).start()
    value_copy(1).start()

    decay_copy.wait()
    stacked = jnp.concatenate([decays[:, pl.ds(i * STRETCH, STRETCH)] for i in range(STEPS)], axis=0)
    cum = running_sums(stacked)
    total = lanes(cum[:, STRETCH - 1 :])
    rest = jnp.exp(twice(total) - cum)
    first = lax.axis_index("ctx") * STEPS
    whole = jnp.zeros((heads, STATE), F32)
    for i in range(STEPS):
        rows = slice(i * heads, (i + 1) * heads)
        tail[:, pl.ds(i * STRETCH, STRETCH)] = rest[rows]
        same = (docs[first + max(i - 1, 0)] == docs[first + i]).astype(F32)
        grow[i] = jnp.exp(total[rows]) * same
        whole = whole + total[rows]
    store_total(pay, heads * HEAD, whole)

    def states(k):
        at = pl.ds(k * BLOCK, BLOCK)
        for h in range(per_block):
            rows = pl.ds(k * BLOCK + h * HEAD, HEAD)
            row = k * per_block + h
            scaled[rows, :] = (v[rows, :].astype(F32) * tail[row : row + 1, :]).astype(BF16)
        run = None
        for i in range(STEPS):
            here = pl.ds(i * STRETCH, STRETCH)
            state = dot(scaled[at, here], sp[here, :STATE])
            if i == 0:
                run = state
                local[0, at, :] = state.astype(BF16)
                continue
            factor = jnp.concatenate(
                [
                    jnp.broadcast_to(grow[i, k * per_block + h : k * per_block + h + 1, :], (HEAD, STATE))
                    for h in range(per_block)
                ],
                axis=0,
            )
            run = run * factor + state
            if i == 1:
                local[1, at, :] = run.astype(BF16)
            if i == 2:
                local[2, at, :] = state.astype(BF16)
        pay[at, :] = run.astype(BF16)

    for k in range(blocks):
        at = pl.ds(k * BLOCK, BLOCK)
        if k:
            value_copy(k).wait()
            for i in range(STEPS):
                here = pl.ds(i * STRETCH, STRETCH)
                v[at, here] = jnp.transpose(dot(tok[here, :], w_value[:, at]).astype(BF16))
            states(k - 1)
        else:
            for i in range(STEPS):
                here = pl.ds(i * STRETCH, STRETCH)
                token_copy(i).wait()
                if i == 0:
                    state_copy.wait()
                sp[here, :] = dot(tok[here, :], w_state[...]).astype(BF16)
                if i == 0:
                    value_copy(0).wait()
                if i == 1:
                    value_copy(2).start()
                if i == 2:
                    value_copy(3).start()
                v[at, here] = jnp.transpose(dot(tok[here, :], w_value[:, at]).astype(BF16))
    states(blocks - 1)


def project(docs, decays, tokens, w_value, w_state):
    rows, depth = tokens.shape
    heads = decays.shape[0]
    width = w_value.shape[1]
    return call(
        project_kernel,
        "project",
        [SMEM, FAR, FAR, FAR, FAR],
        [
            ((rows, depth), BF16),
            ((rows, 2 * STATE), BF16),
            ((width, rows), BF16),
            ((3, width, STATE), BF16),
            ((width + 3 * heads, STATE), BF16),
        ],
        (docs, *(far(x) for x in (decays, tokens, w_value, w_state))),
        [
            pltpu.VMEM((depth, width), BF16),
            pltpu.VMEM((depth, 2 * STATE), BF16),
            pltpu.VMEM((heads, rows), F32),
            pltpu.VMEM((STEPS, heads, STATE), F32),
            pltpu.VMEM((width, rows), BF16),
            pltpu.VMEM((heads, rows), F32),
            pltpu.SemaphoreType.DMA((STEPS + width // BLOCK + 2,)),
        ],
        mib=16,
        flops=2 * rows * depth * (width + 2 * STATE),
        moved=2 * (rows * depth + depth * width),
    )


def joined(docs, last_first, last_second):
    return (docs[last_first] == docs[last_second]).astype(F32)


def half_rows(core, *factors):
    half = factors[0].shape[0] // 2
    return [jnp.where(core == 0, x[:half], x[half:]) for x in factors]


def near_kernel(docs, own, peer, pay, earlier):
    heads = earlier.shape[0]
    half = heads // 2
    ctx = lax.axis_index("ctx")
    core, pair = ctx & 1, ctx >> 1
    second = core == 1
    total_own, total_peer = load_total(own, heads * HEAD, heads), load_total(peer, heads * HEAD, heads)
    keep = joined(docs, pair * 2 * STEPS + STEPS - 1, pair * 2 * STEPS + 2 * STEPS - 1)
    factor = jnp.exp(jnp.where(second, total_own, total_peer)) * keep
    own_by, peer_by = half_rows(core, jnp.where(second, 1.0, factor), jnp.where(second, factor, 1.0))
    for h in range(half):
        at = pl.ds(pl.multiple_of(core * (half * HEAD) + h * HEAD, HEAD), HEAD)
        row = slice(h, h + 1)
        pay[pl.ds(h * HEAD, HEAD), :] = (
            own[at, :].astype(F32) * own_by[row] + peer[at, :].astype(F32) * peer_by[row]
        ).astype(BF16)
    store_total(pay, half * HEAD, total_own + total_peer)
    earlier[...] = jnp.where(second, total_peer, 0.0)


def middle_kernel(docs, own, one, two, three, before, after, pay, left, earlier):
    heads = before.shape[0]
    half = heads // 2
    top = half * HEAD
    ctx = lax.axis_index("ctx")
    core, chip = ctx & 1, ctx >> 1
    odd, high = (chip & 1) == 1, (chip & 2) == 2
    t_own, t_one, t_two, t_three = (load_total(x, top, heads) for x in (own, one, two, three))
    last = lambda at: (at + 1) * 2 * STEPS - 1
    base, mine, theirs = (chip >> 2) << 2, (chip >> 1) << 1, ((chip >> 1) ^ 1) << 1
    keep_mine = joined(docs, last(mine), last(mine + 1))
    keep_theirs = joined(docs, last(theirs), last(theirs + 1))
    keep_all = joined(docs, last(base + 1), last(base + 3))
    by_mine = jnp.exp(jnp.where(odd, t_own, t_one)) * keep_mine
    by_theirs = jnp.exp(jnp.where(odd, t_two, t_three)) * keep_theirs
    by_all = jnp.exp(jnp.where(high, t_own + t_one, t_two + t_three)) * keep_all
    own_by, one_by, two_by, three_by, mine_by, theirs_by = half_rows(
        core,
        jnp.where(odd, 1.0, by_mine),
        jnp.where(odd, by_mine, 1.0),
        jnp.where(odd, 1.0, by_theirs),
        jnp.where(odd, by_theirs, 1.0),
        jnp.where(high, 1.0, by_all),
        jnp.where(high, by_all, 1.0),
    )
    for h in range(half):
        at = pl.ds(h * HEAD, HEAD)
        row = slice(h, h + 1)
        here = own[at, :].astype(F32) * own_by[row] + one[at, :].astype(F32) * one_by[row]
        there = two[at, :].astype(F32) * two_by[row] + three[at, :].astype(F32) * three_by[row]
        left[at, :] = one[at, :]
        left[pl.ds(top + h * HEAD, HEAD), :] = there.astype(BF16)
        pay[at, :] = (here * mine_by[row] + there * theirs_by[row]).astype(BF16)
    store_total(pay, top, (t_own + t_one) + (t_two + t_three))
    second = before[...] + jnp.where(odd, t_one, 0.0)
    earlier[pl.ds(0, heads), :] = second
    earlier[pl.ds(heads, heads), :] = second + jnp.where(high, t_two + t_three, 0.0)


def far_kernel(docs, one, two, three, before, after, left, earlier):
    heads = earlier.shape[0]
    half = heads // 2
    top = half * HEAD
    ctx = lax.axis_index("ctx")
    row_of = ctx >> 3
    odd = (row_of & 1) == 1
    t_one, t_two, t_three = (load_total(x, top, heads) for x in (one, two, three))
    theirs = ((row_of >> 1) ^ 1) << 1
    last = lambda at: (at + 1) * 8 * STEPS - 1
    factor = jnp.exp(jnp.where(odd, t_two, t_three)) * joined(docs, last(theirs), last(theirs + 1))
    two_by, three_by = half_rows(ctx & 1, jnp.where(odd, 1.0, factor), jnp.where(odd, factor, 1.0))
    for h in range(half):
        at = pl.ds(h * HEAD, HEAD)
        row = slice(h, h + 1)
        left[at, :] = one[at, :]
        left[pl.ds(top + h * HEAD, HEAD), :] = (
            two[at, :].astype(F32) * two_by[row] + three[at, :].astype(F32) * three_by[row]
        ).astype(BF16)
    earlier[...] = before[pl.ds(heads, heads), :] + jnp.where(odd, t_one, 0.0)


def assemble(core, own, peer, full):
    half = own.shape[0] // 2
    for level in range(2):
        source = pl.ds(level * half, half)
        full[level, pl.ds(pl.multiple_of(core * half, half), half), :] = own[source, :]
        full[level, pl.ds(pl.multiple_of((1 - core) * half, half), half), :] = peer[source, :]


SEND_ORDER = ((2, 0), (1, 1), (2, 1), (3, 0), (1, 0), (3, 1), (0, 0), (0, 1))


def gate_kernel(tok, w_level, gate_hbm, out_hbm, gates, weight, w_out, w_gate, sems):
    blocks = w_gate.shape[1] // GATE_BLOCK
    tp = lax.axis_index("tp")
    eighth = w_out.shape[1] // len(SEND_ORDER)

    def gate_copy(k):
        at = pl.ds(k * GATE_BLOCK, GATE_BLOCK)
        return pltpu.make_async_copy(gate_hbm.at[:, at], w_gate.at[:, at], sems.at[k])

    def out_copy(j):
        shift, side = SEND_ORDER[j]
        source = pl.ds(pl.multiple_of((((tp + shift) & 3) * 2 + side) * eighth, eighth), eighth)
        return pltpu.make_async_copy(out_hbm.at[:, source], w_out.at[:, pl.ds(j * eighth, eighth)], sems.at[blocks + j])

    for k in range(blocks):
        gate_copy(k).start()
    cols = w_level.shape[1]
    heads = cols // LEVELS
    to_row, from_col = iota((cols, cols), 0), iota((cols, cols), 1)
    pick = ((to_row % heads) * LEVELS + to_row // heads == from_col).astype(BF16)
    turned = dot_nt(pick, dot(tok[...], w_level[...]).astype(BF16))
    weight[...] = jnp.maximum(turned, 0.0) + jnp.log1p(jnp.exp(-jnp.abs(turned)))
    for k in range(blocks):
        gate_copy(k).wait()
        if k == 0:
            for j in range(len(SEND_ORDER)):
                out_copy(j).start()
        at = pl.ds(k * GATE_BLOCK, GATE_BLOCK)
        gates[at, :] = jnp.transpose(dot(tok[...], w_gate[:, at]).astype(BF16))
    for j in range(len(SEND_ORDER)):
        out_copy(j).wait()


def remote_term(docs, ctx, bit, stretch_doc, weight, here, gone, source, c_out):
    heads = weight.shape[0] // LEVELS
    base = (ctx >> (bit + 1)) << (bit + 1)
    last_left = docs[(base + (1 << bit)) * STEPS - 1]
    live = ((((ctx >> bit) & 1) == 1) & (last_left == stretch_doc)).astype(F32)
    rows = weight[pl.ds((bit + 3) * heads, heads), here] * live
    if gone is not None:
        rows = rows * twice(jnp.exp(gone))
    return dot_nt(source[pl.ds(0, heads * HEAD), :], c_out), rows


def intra_kernel(docs, skip, weight, decays, v, sp, local, r0, ho, scaled_weight):
    heads = decays.shape[0]
    ctx = lax.axis_index("ctx")
    first = ctx * STEPS
    causal = iota((128, 128), 0) <= iota((128, 128), 1)
    lower = (iota((STRETCH, STRETCH), 0) >= iota((STRETCH, STRETCH), 1)).astype(BF16)
    begin = jnp.zeros((heads, STATE), F32)
    previous = begin
    for index in range(STEPS):
        here = pl.ds(index * STRETCH, STRETCH)
        now = decays[:, here]
        cum = running_sums(now)
        parts = dot_nt(lower, split(now))
        cum_col = (parts[:, :heads] + parts[:, heads : 2 * heads]) + parts[:, 2 * heads :]
        total = lanes(cum[:, STRETCH - 1 :])
        grown = jnp.exp(cum)
        from_device = jnp.exp(cum + twice(begin))
        for level in range(3, LEVELS):
            rows = pl.ds(level * heads, heads)
            scaled_weight[rows, here] = weight[rows, here] * from_device
        b_in, c_out = sp[here, :STATE], sp[here, STATE:]
        scores = dot_nt(b_in, c_out)
        terms = []
        if index & 1:
            keep = joined(docs, first + index - 1, first + index)
            terms.append((0 if index == 1 else 2, weight[pl.ds(heads, heads), here] * grown * keep))
        if index & 2:
            keep = joined(docs, first + 1, first + index)
            factor = grown * jnp.exp(twice(previous)) if index == 3 else grown
            terms.append((1, weight[pl.ds(2 * heads, heads), here] * factor * keep))
        crosses = [(dot_nt(local[slot], c_out), row) for slot, row in terms]
        stretch_doc = docs[first + index]
        crosses.append(remote_term(docs, ctx, 0, stretch_doc, scaled_weight, here, None, r0, c_out))
        own_weight = weight[pl.ds(0, heads), here]
        for h in range(heads):
            at = slice(h * HEAD, (h + 1) * HEAD)
            col = cum_col[:, h : h + 1]
            row = cum[h : h + 1, :]

            def block(s, t, masked):
                decay = jnp.exp(
                    jnp.broadcast_to(row[:, t * 128 : t * 128 + 128], (128, 128)) - col[s * 128 : s * 128 + 128, :]
                )
                if masked:
                    decay = jnp.where(causal, decay, 0.0)
                return (scores[s * 128 : s * 128 + 128, t * 128 : t * 128 + 128] * decay).astype(BF16)

            vh = v[pl.ds(h * HEAD, HEAD), here]
            left = dot(vh[:, :128], block(0, 0, True))
            right = dot(vh, jnp.concatenate([block(0, 1, False), block(1, 1, True)], axis=0))
            out = skip[h] * vh.astype(F32) + own_weight[h : h + 1, :] * jnp.concatenate([left, right], axis=1)
            for cross, factor in crosses:
                out = out + factor[h : h + 1, :] * cross[at]
            ho[pl.ds(h * HEAD, HEAD), here] = out
        begin = begin + total
        previous = total


def late_kernel(docs, sp, ho, weight, e1, e23, own, peer, out, full):
    heads = e1.shape[0]
    ctx = lax.axis_index("ctx")
    assemble(ctx & 1, own, peer, full)
    for index in range(STEPS):
        here = pl.ds(index * STRETCH, STRETCH)
        c_out = sp[here, STATE:]
        stretch_doc = docs[ctx * STEPS + index]
        terms = [
            remote_term(docs, ctx, bit, stretch_doc, weight, here, gone, full.at[bit - 1], c_out)
            for bit, gone in ((1, e1[...]), (2, e23[pl.ds(0, heads), :]))
        ]
        for h in range(heads):
            at = pl.ds(h * HEAD, HEAD)
            total = ho[at, here]
            for cross, rows in terms:
                total = total + rows[h : h + 1, :] * cross[h * HEAD : (h + 1) * HEAD]
            out[at, here] = total


def finish_kernel(
    start, count, docs, gain, w_out, sp, gates, ho, weight, e23, e4, *refs
):
    far_own, far_peer, plus, minus, normed, acc, full = refs
    ctx = lax.axis_index("ctx")
    heads = e4.shape[0]
    assemble(ctx & 1, far_own, far_peer, full)
    for j in range(count):
        here = pl.ds((start + j) * STRETCH, STRETCH)
        c_out = sp[here, STATE:]
        stretch_doc = docs[ctx * STEPS + start + j]
        terms = [
            remote_term(docs, ctx, bit, stretch_doc, weight, here, gone, full.at[bit - 3], c_out)
            for bit, gone in ((3, e23[pl.ds(heads, heads), :]), (4, e4[...]))
        ]
        for h in range(heads):
            at = pl.ds(h * HEAD, HEAD)
            total = ho[at, here]
            for cross, rows in terms:
                total = total + rows[h : h + 1, :] * cross[h * HEAD : (h + 1) * HEAD]
            g = gates[at, here].astype(F32)
            gated = total * (g / (1.0 + jnp.exp(-g)))
            power = jnp.sum(gated * gated, axis=0, keepdims=True) * (1.0 / HEAD)
            acc[at, :] = gated * lax.rsqrt(power + 1e-5)
        normed[pl.ds(j * STRETCH, STRETCH), :] = (jnp.transpose(acc[...]) * gain[...]).astype(BF16)
    quarter = w_out.shape[1] // 4
    for j, out in enumerate((plus, minus)):
        out[...] = dot(normed[...], w_out[:, pl.ds(j * quarter, quarter)]).astype(BF16)


def stay_kernel(normed, w_out, keep, own):
    quarter = w_out.shape[1] // 4
    for j, out in enumerate((keep, own)):
        out[...] = dot(normed[...], w_out[:, pl.ds((j + 2) * quarter, quarter)]).astype(BF16)


def stay(start, normed, w_out):
    rows, width = normed.shape
    depth = w_out.shape[1]
    return call(
        stay_kernel,
        f"stay{start}",
        [VMEM] * 2,
        [((rows, depth // 4), BF16)] * 2,
        (normed, w_out),
        mib=8,
        flops=rows * depth * width,
        moved=1 << 20,
    )


def finish(start, stop, docs, gain, w_out, *operands):
    count = stop - start
    width, depth = w_out.shape
    rows = count * STRETCH
    return call(
        functools.partial(finish_kernel, start, count),
        f"finish{start}",
        [SMEM] + [VMEM] * (2 + len(operands)),
        [((rows, depth // 4), BF16)] * 2 + [((rows, width), BF16)],
        (docs, gain, w_out, *operands),
        [
            pltpu.VMEM((width, STRETCH), F32),
            pltpu.VMEM((2, width, STATE), BF16),
        ],
        mib=16,
        flops=2 * rows * depth * width,
        moved=2 * width * depth + 8 * rows * width,
    )


def per_device(tokens, w_value, w_gate, w_state, w_level, log_decay, skip_weight, norm_gain, doc_ids, w_out):
    rows, depth = tokens.shape
    width = w_value.shape[1]
    heads = log_decay.shape[1]
    docs = far(doc_ids)
    decays = jnp.transpose(log_decay)
    part = ((width // 2 + 3 * heads, STATE), BF16)
    tail = ((width, STATE), BF16)
    gone = ((heads, STATE), F32)

    def across(x, by):
        return lax.ppermute(x, "ctx", [(i, i ^ by) for i in range(32)])

    def turn(x, by):
        return lax.ppermute(x, "tp", [(i, (i + by) % 4) for i in range(4)])

    tok, sp, v, local, pay0 = project(docs, decays, tokens, w_value, w_state)
    peer = across(pay0, 1)
    pay1, e1 = call(
        near_kernel, "near", [SMEM] + [VMEM] * 2, [part, gone], (docs, pay0, peer)
    )
    ys = [across(pay1, by) for by in (4, 2, 6)]
    gates, weight, w_out_near = call(
        gate_kernel,
        "gate",
        [VMEM] * 2 + [FAR] * 2,
        [((width, rows), BF16), ((heads * LEVELS, rows), F32), (w_out.shape, BF16)],
        (tok, w_level, far(w_gate), far(w_out)),
        [pltpu.VMEM(w_gate.shape, BF16), pltpu.SemaphoreType.DMA((width // GATE_BLOCK + len(SEND_ORDER),))],
        mib=16,
        flops=2 * rows * depth * (width + STATE),
        moved=2 * (rows * depth + depth * width),
    )
    y2, y1, y3 = ys
    pay2, mid_own, e23 = call(
        middle_kernel,
        "middle",
        [SMEM] + [VMEM] * 6,
        [part, tail, ((2 * heads, STATE), F32)],
        (docs, pay1, y1, y2, y3, e1, weight),
    )
    x2, x1, x3 = (across(pay2, by) for by in (16, 8, 24))
    mid_peer = across(mid_own, 1)
    ho, scaled_weight = call(
        intra_kernel,
        "intra",
        [SMEM] * 2 + [VMEM] * 6,
        [((width, rows), F32), ((heads * LEVELS, rows), F32)],
        (docs, skip_weight, weight, decays, v, sp, local, peer),
        mib=12,
        flops=6 << 30,
        moved=8 << 20,
    )
    far_own, e4 = call(
        far_kernel,
        "far",
        [SMEM] + [VMEM] * 5,
        [tail, gone],
        (docs, x1, x2, x3, e23, scaled_weight),
    )
    far_peer = across(far_own, 1)
    (ho,) = call(
        late_kernel,
        "late",
        [SMEM] + [VMEM] * 7,
        [((width, rows), F32)],
        (docs, sp, ho, scaled_weight, e1, e23, mid_own, mid_peer),
        [pltpu.VMEM((2, width, STATE), BF16)],
        mib=8,
        flops=2 << 30,
        moved=4 << 20,
    )
    gain = norm_gain.reshape(1, -1)
    results = []
    half = w_out.shape[1] // 8
    for lo, hi in CHUNKS:
        plus, minus, normed = finish(
            lo, hi, docs, gain, w_out_near, sp, gates, ho, scaled_weight, e23, e4, far_own, far_peer
        )
        from_below, from_above = turn(plus, 1), turn(minus, 3)
        keep, own = stay(lo, normed, w_out_near)
        on_plus = (keep[:, :half].astype(F32) + from_below[:, :half].astype(F32)).astype(BF16)
        on_minus = (keep[:, half:].astype(F32) + from_above[:, :half].astype(F32)).astype(BF16)
        last_below, last_above = turn(on_plus, 1), turn(on_minus, 3)
        first = own[:, :half].astype(F32) + from_above[:, half:].astype(F32) + last_below.astype(F32)
        second = own[:, half:].astype(F32) + from_below[:, half:].astype(F32) + last_above.astype(F32)
        results.append(jnp.concatenate([first, second], axis=1).astype(BF16))
    return jnp.concatenate(results, axis=0)


def solution(mesh):
    placed = (
        P("ctx", None),
        P(None, "tp"),
        P(None, "tp"),
        P(),
        P(None, "tp"),
        P("ctx", "tp"),
        P("tp"),
        P("tp"),
        P(),
        P("tp", None),
    )
    return jax.shard_map(per_device, mesh=mesh, in_specs=placed, out_specs=P("ctx", "tp"), check_vma=False)
```

```python
import functools

import jax
import jax.numpy as jnp
from jax import lax
from jax.experimental import pallas as pl
from jax.experimental.pallas import tpu as pltpu
from jax.sharding import PartitionSpec as P

STRETCH = 256
STEPS = 4
HEAD = 64
STATE = 128
LEVELS = 8
LATE_FROM = 2
BLOCK = 256
GATE_BLOCK = 512
F32 = jnp.float32
BF16 = jnp.bfloat16
NT = (((1,), (1,)), ((), ()))
CHUNKS = ((0, 2), (2, 3), (3, 4))
SMEM = pl.BlockSpec(memory_space=pltpu.SMEM)
VMEM = pl.BlockSpec(memory_space=pltpu.VMEM)
FAR = pl.BlockSpec(memory_space=pltpu.HBM)


def dot(a, b):
    return jnp.dot(a, b, preferred_element_type=F32)


def dot_nt(a, b):
    return lax.dot_general(a, b, NT, preferred_element_type=F32)


def iota(shape, dim):
    return lax.broadcasted_iota(jnp.int32, shape, dim)


def far(x):
    return pltpu.with_memory_space_constraint(x, pltpu.HBM)


def twice(x):
    return jnp.concatenate([x, x], axis=1)


def split(x):
    high = x.astype(BF16)
    rest = x - high.astype(F32)
    middle = rest.astype(BF16)
    low = (rest - middle.astype(F32)).astype(BF16)
    return jnp.concatenate([high, middle, low], axis=0)


def running_sums(decays):
    rows = decays.shape[0]
    shape = (STRETCH, STRETCH)
    parts = dot(split(decays), (iota(shape, 0) <= iota(shape, 1)).astype(BF16))
    return (parts[:rows] + parts[rows : 2 * rows]) + parts[2 * rows :]


def lanes(column):
    return jnp.broadcast_to(column, (column.shape[0], STATE))


def store_total(ref, top, total):
    heads = total.shape[0]
    high = total.astype(BF16)
    rest = total - high.astype(F32)
    middle = rest.astype(BF16)
    low = (rest - middle.astype(F32)).astype(BF16)
    ref[pl.ds(top, heads), :] = high
    ref[pl.ds(top + heads, heads), :] = middle
    ref[pl.ds(top + 2 * heads, heads), :] = low


def load_total(ref, top, heads):
    parts = [ref[pl.ds(top + k * heads, heads), :].astype(F32) for k in range(3)]
    return (parts[0] + parts[1]) + parts[2]


def call(kernel, name, in_specs, out_shape, args, scratch=(), mib=8, flops=1 << 20, moved=1 << 20, out_specs=None):
    return pl.pallas_call(
        kernel,
        name=name,
        in_specs=in_specs,
        out_specs=[VMEM] * len(out_shape),
        out_shape=[jax.ShapeDtypeStruct(*x) for x in out_shape],
        scratch_shapes=list(scratch),
        compiler_params=pltpu.CompilerParams(vmem_limit_bytes=mib << 20),
        cost_estimate=pl.CostEstimate(flops=flops, bytes_accessed=moved, transcendentals=0),
    )(*args)


def project_kernel(
    docs, decays_hbm, tok_hbm, value_hbm, state_hbm, tok, sp, v, local, pay, w_value, w_state, tail, grow, scaled, decays,
    sems,
):
    heads = decays.shape[0]
    blocks = w_value.shape[1] // BLOCK
    per_block = BLOCK // HEAD

    def token_copy(i):
        at = pl.ds(i * STRETCH, STRETCH)
        return pltpu.make_async_copy(tok_hbm.at[at, :], tok.at[at, :], sems.at[i])

    def value_copy(k):
        at = pl.ds(k * BLOCK, BLOCK)
        return pltpu.make_async_copy(value_hbm.at[:, at], w_value.at[:, at], sems.at[STEPS + k])

    state_copy = pltpu.make_async_copy(state_hbm, w_state, sems.at[STEPS + blocks])
    decay_copy = pltpu.make_async_copy(decays_hbm, decays, sems.at[STEPS + blocks + 1])
    decay_copy.start()
    token_copy(0).start()
    state_copy.start()
    value_copy(0).start()
    for i in range(1, STEPS):
        token_copy(i).start()
    value_copy(1).start()

    decay_copy.wait()
    stacked = jnp.concatenate([decays[:, pl.ds(i * STRETCH, STRETCH)] for i in range(STEPS)], axis=0)
    cum = running_sums(stacked)
    total = lanes(cum[:, STRETCH - 1 :])
    rest = jnp.exp(twice(total) - cum)
    first = lax.axis_index("ctx") * STEPS
    whole = jnp.zeros((heads, STATE), F32)
    for i in range(STEPS):
        rows = slice(i * heads, (i + 1) * heads)
        tail[:, pl.ds(i * STRETCH, STRETCH)] = rest[rows]
        same = (docs[first + max(i - 1, 0)] == docs[first + i]).astype(F32)
        grow[i] = jnp.exp(total[rows]) * same
        whole = whole + total[rows]
    store_total(pay, heads * HEAD, whole)

    def states(k):
        at = pl.ds(k * BLOCK, BLOCK)
        for h in range(per_block):
            rows = pl.ds(k * BLOCK + h * HEAD, HEAD)
            row = k * per_block + h
            scaled[rows, :] = (v[rows, :].astype(F32) * tail[row : row + 1, :]).astype(BF16)
        run = None
        for i in range(STEPS):
            here = pl.ds(i * STRETCH, STRETCH)
            state = dot(scaled[at, here], sp[here, :STATE])
            if i == 0:
                run = state
                local[0, at, :] = state.astype(BF16)
                continue
            factor = jnp.concatenate(
                [
                    jnp.broadcast_to(grow[i, k * per_block + h : k * per_block + h + 1, :], (HEAD, STATE))
                    for h in range(per_block)
                ],
                axis=0,
            )
            run = run * factor + state
            if i == 1:
                local[1, at, :] = run.astype(BF16)
            if i == 2:
                local[2, at, :] = state.astype(BF16)
        pay[at, :] = run.astype(BF16)

    for k in range(blocks):
        at = pl.ds(k * BLOCK, BLOCK)
        if k:
            value_copy(k).wait()
            for i in range(STEPS):
                here = pl.ds(i * STRETCH, STRETCH)
                v[at, here] = jnp.transpose(dot(tok[here, :], w_value[:, at]).astype(BF16))
            states(k - 1)
        else:
            for i in range(STEPS):
                here = pl.ds(i * STRETCH, STRETCH)
                token_copy(i).wait()
                if i == 0:
                    state_copy.wait()
                sp[here, :] = dot(tok[here, :], w_state[...]).astype(BF16)
                if i == 0:
                    value_copy(0).wait()
                if i == 1:
                    value_copy(2).start()
                if i == 2:
                    value_copy(3).start()
                v[at, here] = jnp.transpose(dot(tok[here, :], w_value[:, at]).astype(BF16))
    states(blocks - 1)


def project(docs, decays, tokens, w_value, w_state):
    rows, depth = tokens.shape
    heads = decays.shape[0]
    width = w_value.shape[1]
    return call(
        project_kernel,
        "project",
        [SMEM, FAR, FAR, FAR, FAR],
        [
            ((rows, depth), BF16),
            ((rows, 2 * STATE), BF16),
            ((width, rows), BF16),
            ((3, width, STATE), BF16),
            ((width + 3 * heads, STATE), BF16),
        ],
        (docs, *(far(x) for x in (decays, tokens, w_value, w_state))),
        [
            pltpu.VMEM((depth, width), BF16),
            pltpu.VMEM((depth, 2 * STATE), BF16),
            pltpu.VMEM((heads, rows), F32),
            pltpu.VMEM((STEPS, heads, STATE), F32),
            pltpu.VMEM((width, rows), BF16),
            pltpu.VMEM((heads, rows), F32),
            pltpu.SemaphoreType.DMA((STEPS + width // BLOCK + 2,)),
        ],
        mib=16,
        flops=2 * rows * depth * (width + 2 * STATE),
        moved=2 * (rows * depth + depth * width),
    )


def joined(docs, last_first, last_second):
    return (docs[last_first] == docs[last_second]).astype(F32)


def half_rows(core, *factors):
    half = factors[0].shape[0] // 2
    return [jnp.where(core == 0, x[:half], x[half:]) for x in factors]


def near_kernel(docs, own, peer, pay, earlier):
    heads = earlier.shape[0]
    half = heads // 2
    ctx = lax.axis_index("ctx")
    core, pair = ctx & 1, ctx >> 1
    second = core == 1
    total_own, total_peer = load_total(own, heads * HEAD, heads), load_total(peer, heads * HEAD, heads)
    keep = joined(docs, pair * 2 * STEPS + STEPS - 1, pair * 2 * STEPS + 2 * STEPS - 1)
    factor = jnp.exp(jnp.where(second, total_own, total_peer)) * keep
    own_by, peer_by = half_rows(core, jnp.where(second, 1.0, factor), jnp.where(second, factor, 1.0))
    for h in range(half):
        at = pl.ds(pl.multiple_of(core * (half * HEAD) + h * HEAD, HEAD), HEAD)
        row = slice(h, h + 1)
        pay[pl.ds(h * HEAD, HEAD), :] = (
            own[at, :].astype(F32) * own_by[row] + peer[at, :].astype(F32) * peer_by[row]
        ).astype(BF16)
    store_total(pay, half * HEAD, total_own + total_peer)
    earlier[...] = jnp.where(second, total_peer, 0.0)


def middle_kernel(docs, own, one, two, three, before, after, pay, left, earlier):
    heads = before.shape[0]
    half = heads // 2
    top = half * HEAD
    ctx = lax.axis_index("ctx")
    core, chip = ctx & 1, ctx >> 1
    odd, high = (chip & 1) == 1, (chip & 2) == 2
    t_own, t_one, t_two, t_three = (load_total(x, top, heads) for x in (own, one, two, three))
    last = lambda at: (at + 1) * 2 * STEPS - 1
    base, mine, theirs = (chip >> 2) << 2, (chip >> 1) << 1, ((chip >> 1) ^ 1) << 1
    keep_mine = joined(docs, last(mine), last(mine + 1))
    keep_theirs = joined(docs, last(theirs), last(theirs + 1))
    keep_all = joined(docs, last(base + 1), last(base + 3))
    by_mine = jnp.exp(jnp.where(odd, t_own, t_one)) * keep_mine
    by_theirs = jnp.exp(jnp.where(odd, t_two, t_three)) * keep_theirs
    by_all = jnp.exp(jnp.where(high, t_own + t_one, t_two + t_three)) * keep_all
    own_by, one_by, two_by, three_by, mine_by, theirs_by = half_rows(
        core,
        jnp.where(odd, 1.0, by_mine),
        jnp.where(odd, by_mine, 1.0),
        jnp.where(odd, 1.0, by_theirs),
        jnp.where(odd, by_theirs, 1.0),
        jnp.where(high, 1.0, by_all),
        jnp.where(high, by_all, 1.0),
    )
    for h in range(half):
        at = pl.ds(h * HEAD, HEAD)
        row = slice(h, h + 1)
        here = own[at, :].astype(F32) * own_by[row] + one[at, :].astype(F32) * one_by[row]
        there = two[at, :].astype(F32) * two_by[row] + three[at, :].astype(F32) * three_by[row]
        left[at, :] = one[at, :]
        left[pl.ds(top + h * HEAD, HEAD), :] = there.astype(BF16)
        pay[at, :] = (here * mine_by[row] + there * theirs_by[row]).astype(BF16)
    store_total(pay, top, (t_own + t_one) + (t_two + t_three))
    second = before[...] + jnp.where(odd, t_one, 0.0)
    earlier[pl.ds(0, heads), :] = second
    earlier[pl.ds(heads, heads), :] = second + jnp.where(high, t_two + t_three, 0.0)


def far_kernel(docs, one, two, three, before, after, left, earlier):
    heads = earlier.shape[0]
    half = heads // 2
    top = half * HEAD
    ctx = lax.axis_index("ctx")
    row_of = ctx >> 3
    odd = (row_of & 1) == 1
    t_one, t_two, t_three = (load_total(x, top, heads) for x in (one, two, three))
    theirs = ((row_of >> 1) ^ 1) << 1
    last = lambda at: (at + 1) * 8 * STEPS - 1
    factor = jnp.exp(jnp.where(odd, t_two, t_three)) * joined(docs, last(theirs), last(theirs + 1))
    two_by, three_by = half_rows(ctx & 1, jnp.where(odd, 1.0, factor), jnp.where(odd, factor, 1.0))
    for h in range(half):
        at = pl.ds(h * HEAD, HEAD)
        row = slice(h, h + 1)
        left[at, :] = one[at, :]
        left[pl.ds(top + h * HEAD, HEAD), :] = (
            two[at, :].astype(F32) * two_by[row] + three[at, :].astype(F32) * three_by[row]
        ).astype(BF16)
    earlier[...] = before[pl.ds(heads, heads), :] + jnp.where(odd, t_one, 0.0)


def assemble(core, own, peer, full):
    half = own.shape[0] // 2
    for level in range(2):
        source = pl.ds(level * half, half)
        full[level, pl.ds(pl.multiple_of(core * half, half), half), :] = own[source, :]
        full[level, pl.ds(pl.multiple_of((1 - core) * half, half), half), :] = peer[source, :]


SEND_ORDER = ((2, 0), (1, 1), (2, 1), (3, 0), (1, 0), (3, 1), (0, 0), (0, 1))


def gate_kernel(tok, w_level, gate_hbm, out_hbm, gates, weight, w_out, w_gate, sems):
    now = pl.ds(STRETCH, tok.shape[0] - STRETCH)
    blocks = w_gate.shape[1] // GATE_BLOCK
    tp = lax.axis_index("tp")
    eighth = w_out.shape[1] // len(SEND_ORDER)

    def gate_copy(k):
        at = pl.ds(k * GATE_BLOCK, GATE_BLOCK)
        return pltpu.make_async_copy(gate_hbm.at[:, at], w_gate.at[:, at], sems.at[k])

    def out_copy(j):
        shift, side = SEND_ORDER[j]
        source = pl.ds(pl.multiple_of((((tp + shift) & 3) * 2 + side) * eighth, eighth), eighth)
        return pltpu.make_async_copy(out_hbm.at[:, source], w_out.at[:, pl.ds(j * eighth, eighth)], sems.at[blocks + j])

    for k in range(blocks):
        gate_copy(k).start()
    cols = w_level.shape[1]
    heads = cols // LEVELS
    to_row, from_col = iota((cols, cols), 0), iota((cols, cols), 1)
    pick = ((to_row % heads) * LEVELS + to_row // heads == from_col).astype(BF16)
    turned = dot_nt(pick, dot(tok[...], w_level[...]).astype(BF16))
    weight[...] = jnp.maximum(turned, 0.0) + jnp.log1p(jnp.exp(-jnp.abs(turned)))
    for k in range(blocks):
        gate_copy(k).wait()
        if k == 0:
            for j in range(len(SEND_ORDER)):
                out_copy(j).start()
        at = pl.ds(k * GATE_BLOCK, GATE_BLOCK)
        gates[at, now] = jnp.transpose(dot(tok[now, :], w_gate[:, at]).astype(BF16))
    for j in range(len(SEND_ORDER)):
        out_copy(j).wait()


def first_gate_kernel(tok, w_gate, after, gates):
    for k in range(w_gate.shape[1] // GATE_BLOCK):
        at = pl.ds(k * GATE_BLOCK, GATE_BLOCK)
        gates[at, :] = jnp.transpose(dot(tok[pl.ds(0, STRETCH), :], w_gate[:, at]).astype(BF16))


def remote_term(docs, ctx, bit, stretch_doc, weight, here, gone, source, c_out):
    heads = weight.shape[0] // LEVELS
    base = (ctx >> (bit + 1)) << (bit + 1)
    last_left = docs[(base + (1 << bit)) * STEPS - 1]
    live = ((((ctx >> bit) & 1) == 1) & (last_left == stretch_doc)).astype(F32)
    rows = weight[pl.ds((bit + 3) * heads, heads), here] * live
    if gone is not None:
        rows = rows * twice(jnp.exp(gone))
    return dot_nt(source[pl.ds(0, heads * HEAD), :], c_out), rows


def intra_kernel(docs, skip, weight, decays, v, sp, local, r0, *refs):
    late = len(refs) == 3
    (scaled_weight, _, ho) = refs if late else (refs[1], None, refs[0])
    heads = decays.shape[0]
    ctx = lax.axis_index("ctx")
    first = ctx * STEPS
    causal = iota((128, 128), 0) <= iota((128, 128), 1)
    lower = (iota((STRETCH, STRETCH), 0) >= iota((STRETCH, STRETCH), 1)).astype(BF16)
    begin = jnp.zeros((heads, STATE), F32)
    previous = begin
    for index in range(1 if late else STEPS):
        here = pl.ds(index * STRETCH, STRETCH)
        now = decays[:, here]
        cum = running_sums(now)
        parts = dot_nt(lower, split(now))
        cum_col = (parts[:, :heads] + parts[:, heads : 2 * heads]) + parts[:, 2 * heads :]
        total = lanes(cum[:, STRETCH - 1 :])
        grown = jnp.exp(cum)
        from_device = jnp.exp(cum + twice(begin))
        if not late:
            for level in range(3, LEVELS):
                rows = pl.ds(level * heads, heads)
                scaled_weight[rows, here] = weight[rows, here] * from_device
        if not late and index == 0:
            begin = previous = total
            continue
        b_in, c_out = sp[here, :STATE], sp[here, STATE:]
        scores = dot_nt(b_in, c_out)
        terms = []
        if index & 1:
            keep = joined(docs, first + index - 1, first + index)
            terms.append((0 if index == 1 else 2, weight[pl.ds(heads, heads), here] * grown * keep))
        if index & 2:
            keep = joined(docs, first + 1, first + index)
            factor = grown * jnp.exp(twice(previous)) if index == 3 else grown
            terms.append((1, weight[pl.ds(2 * heads, heads), here] * factor * keep))
        crosses = [(dot_nt(local[slot], c_out), row) for slot, row in terms]
        stretch_doc = docs[first + index]
        crosses.append(remote_term(docs, ctx, 0, stretch_doc, scaled_weight, here, None, r0, c_out))
        own_weight = weight[pl.ds(0, heads), here]
        for h in range(heads):
            at = slice(h * HEAD, (h + 1) * HEAD)
            col = cum_col[:, h : h + 1]
            row = cum[h : h + 1, :]

            def block(s, t, masked):
                decay = jnp.exp(
                    jnp.broadcast_to(row[:, t * 128 : t * 128 + 128], (128, 128)) - col[s * 128 : s * 128 + 128, :]
                )
                if masked:
                    decay = jnp.where(causal, decay, 0.0)
                return (scores[s * 128 : s * 128 + 128, t * 128 : t * 128 + 128] * decay).astype(BF16)

            vh = v[pl.ds(h * HEAD, HEAD), here]
            left = dot(vh[:, :128], block(0, 0, True))
            right = dot(vh, jnp.concatenate([block(0, 1, False), block(1, 1, True)], axis=0))
            out = skip[h] * vh.astype(F32) + own_weight[h : h + 1, :] * jnp.concatenate([left, right], axis=1)
            for cross, factor in crosses:
                out = out + factor[h : h + 1, :] * cross[at]
            ho[pl.ds(h * HEAD, HEAD), here] = out
        begin = begin + total
        previous = total


def late_kernel(docs, sp, ho, weight, e1, e23, own, peer, out, full):
    first = LATE_FROM
    heads = e1.shape[0]
    ctx = lax.axis_index("ctx")
    assemble(ctx & 1, own, peer, full)
    for index in range(first, STEPS):
        here = pl.ds(index * STRETCH, STRETCH)
        c_out = sp[here, STATE:]
        stretch_doc = docs[ctx * STEPS + index]
        terms = [
            remote_term(docs, ctx, bit, stretch_doc, weight, here, gone, full.at[bit - 1], c_out)
            for bit, gone in ((1, e1[...]), (2, e23[pl.ds(0, heads), :]))
        ]
        for h in range(heads):
            at = pl.ds(h * HEAD, HEAD)
            total = ho[at, here]
            for cross, rows in terms:
                total = total + rows[h : h + 1, :] * cross[h * HEAD : (h + 1) * HEAD]
            out[at, here] = total


def finish_kernel(
    start, count, docs, gain, w_out, sp, gates, ho, weight, e23, e4, *refs
):
    far_own, far_peer, *before, plus, minus, normed, acc, full = refs[: len(refs) - (1 if len(refs) > 7 else 0)]
    mid = refs[-1] if before else None
    ctx = lax.axis_index("ctx")
    heads = e4.shape[0]
    assemble(ctx & 1, far_own, far_peer, full)
    if before:
        first_gates, first_ho, mid_own, mid_peer, e1 = before
        assemble(ctx & 1, mid_own, mid_peer, mid)
    for j in range(count):
        at_first = before and start + j == 0
        here = pl.ds((start + j) * STRETCH, STRETCH)
        c_out = sp[here, STATE:]
        stretch_doc = docs[ctx * STEPS + start + j]
        terms = [
            remote_term(docs, ctx, bit, stretch_doc, weight, here, gone, full.at[bit - 3], c_out)
            for bit, gone in ((3, e23[pl.ds(heads, heads), :]), (4, e4[...]))
        ]
        if before:
            terms += [
                remote_term(docs, ctx, bit, stretch_doc, weight, here, gone, mid.at[bit - 1], c_out)
                for bit, gone in ((1, e1[...]), (2, e23[pl.ds(0, heads), :]))
            ]
        for h in range(heads):
            at = pl.ds(h * HEAD, HEAD)
            total = first_ho[at, :] if at_first else ho[at, here]
            for cross, rows in terms:
                total = total + rows[h : h + 1, :] * cross[h * HEAD : (h + 1) * HEAD]
            g = (first_gates[at, :] if at_first else gates[at, here]).astype(F32)
            gated = total * (g / (1.0 + jnp.exp(-g)))
            power = jnp.sum(gated * gated, axis=0, keepdims=True) * (1.0 / HEAD)
            acc[at, :] = gated * lax.rsqrt(power + 1e-5)
        normed[pl.ds(j * STRETCH, STRETCH), :] = (jnp.transpose(acc[...]) * gain[...]).astype(BF16)
    quarter = w_out.shape[1] // 4
    for j, out in enumerate((plus, minus)):
        out[...] = dot(normed[...], w_out[:, pl.ds(j * quarter, quarter)]).astype(BF16)


def stay_kernel(normed, w_out, keep, own):
    quarter = w_out.shape[1] // 4
    for j, out in enumerate((keep, own)):
        out[...] = dot(normed[...], w_out[:, pl.ds((j + 2) * quarter, quarter)]).astype(BF16)


def stay(start, normed, w_out):
    rows, width = normed.shape
    depth = w_out.shape[1]
    return call(
        stay_kernel,
        f"stay{start}",
        [VMEM] * 2,
        [((rows, depth // 4), BF16)] * 2,
        (normed, w_out),
        mib=8,
        flops=rows * depth * width,
        moved=1 << 20,
    )


def finish(start, stop, docs, gain, w_out, *operands):
    count = stop - start
    width, depth = w_out.shape
    rows = count * STRETCH
    return call(
        functools.partial(finish_kernel, start, count),
        f"finish{start}",
        [SMEM] + [VMEM] * (2 + len(operands)),
        [((rows, depth // 4), BF16)] * 2 + [((rows, width), BF16)],
        (docs, gain, w_out, *operands),
        [
            pltpu.VMEM((width, STRETCH), F32),
            pltpu.VMEM((2, width, STATE), BF16),
            *([pltpu.VMEM((2, width, STATE), BF16)] if start < LATE_FROM else []),
        ],
        mib=16,
        flops=2 * rows * depth * width,
        moved=2 * width * depth + 8 * rows * width,
    )


def per_device(tokens, w_value, w_gate, w_state, w_level, log_decay, skip_weight, norm_gain, doc_ids, w_out):
    rows, depth = tokens.shape
    width = w_value.shape[1]
    heads = log_decay.shape[1]
    docs = far(doc_ids)
    decays = jnp.transpose(log_decay)
    part = ((width // 2 + 3 * heads, STATE), BF16)
    tail = ((width, STATE), BF16)
    gone = ((heads, STATE), F32)

    def across(x, by):
        return lax.ppermute(x, "ctx", [(i, i ^ by) for i in range(32)])

    def turn(x, by):
        return lax.ppermute(x, "tp", [(i, (i + by) % 4) for i in range(4)])

    tok, sp, v, local, pay0 = project(docs, decays, tokens, w_value, w_state)
    peer = across(pay0, 1)
    pay1, e1 = call(
        near_kernel, "near", [SMEM] + [VMEM] * 2, [part, gone], (docs, pay0, peer)
    )
    ys = [across(pay1, by) for by in (4, 2, 6)]
    gates, weight, w_out_near, w_gate_near = call(
        gate_kernel,
        "gate",
        [VMEM] * 2 + [FAR] * 2,
        [((width, rows), BF16), ((heads * LEVELS, rows), F32), (w_out.shape, BF16), (w_gate.shape, BF16)],
        (tok, w_level, far(w_gate), far(w_out)),
        [pltpu.SemaphoreType.DMA((width // GATE_BLOCK + len(SEND_ORDER),))],
        mib=16,
        flops=2 * rows * depth * (width + STATE),
        moved=2 * (rows * depth + depth * width),
    )
    y2, y1, y3 = ys
    pay2, mid_own, e23 = call(
        middle_kernel,
        "middle",
        [SMEM] + [VMEM] * 6,
        [part, tail, ((2 * heads, STATE), F32)],
        (docs, pay1, y1, y2, y3, e1, weight),
    )
    x2, x1, x3 = (across(pay2, by) for by in (16, 8, 24))
    mid_peer = across(mid_own, 1)
    ho, scaled_weight = call(
        intra_kernel,
        "intra",
        [SMEM] * 2 + [VMEM] * 6,
        [((width, rows), F32), ((heads * LEVELS, rows), F32)],
        (docs, skip_weight, weight, decays, v, sp, local, peer),
        mib=12,
        flops=6 << 30,
        moved=8 << 20,
    )
    far_own, e4 = call(
        far_kernel,
        "far",
        [SMEM] + [VMEM] * 5,
        [tail, gone],
        (docs, x1, x2, x3, e23, scaled_weight),
    )
    far_peer = across(far_own, 1)
    (ho_late,) = call(
        late_kernel,
        "late",
        [SMEM] + [VMEM] * 7,
        [((width, rows), F32)],
        (docs, sp, ho, scaled_weight, e1, e23, mid_own, mid_peer),
        [pltpu.VMEM((2, width, STATE), BF16)],
        mib=8,
        flops=2 << 30,
        moved=4 << 20,
    )
    gain = norm_gain.reshape(1, -1)
    results, arrived = {}, None
    half = w_out.shape[1] // 8
    for lo, hi in reversed(CHUNKS):
        extra = ()
        if lo < LATE_FROM:
            (first_gates,) = call(
                first_gate_kernel,
                "first_gate",
                [VMEM] * 3,
                [((width, STRETCH), BF16)],
                (tok, w_gate_near, arrived),
                mib=6,
                flops=2 * STRETCH * depth * width,
            )
            (first_ho,) = call(
                intra_kernel,
                "first_intra",
                [SMEM] * 2 + [VMEM] * 8,
                [((width, STRETCH), F32)],
                (docs, skip_weight, weight, decays, v, sp, local, peer, scaled_weight, arrived),
                mib=8,
                flops=1 << 30,
            )
            extra = (first_gates, first_ho, mid_own, mid_peer, e1)
        plus, minus, normed = finish(
            lo, hi, docs, gain, w_out_near, sp, gates, ho_late if lo >= LATE_FROM else ho, scaled_weight,
            e23, e4, far_own, far_peer, *extra,
        )
        from_below, from_above = turn(plus, 1), turn(minus, 3)
        arrived = from_below if arrived is None else arrived
        keep, own = stay(lo, normed, w_out_near)
        on_plus = (keep[:, :half].astype(F32) + from_below[:, :half].astype(F32)).astype(BF16)
        on_minus = (keep[:, half:].astype(F32) + from_above[:, :half].astype(F32)).astype(BF16)
        last_below, last_above = turn(on_plus, 1), turn(on_minus, 3)
        first = own[:, :half].astype(F32) + from_above[:, half:].astype(F32) + last_below.astype(F32)
        second = own[:, half:].astype(F32) + from_below[:, half:].astype(F32) + last_above.astype(F32)
        results[lo] = jnp.concatenate([first, second], axis=1).astype(BF16)
    return jnp.concatenate([results[lo] for lo, _ in CHUNKS], axis=0)


def solution(mesh):
    placed = (
        P("ctx", None),
        P(None, "tp"),
        P(None, "tp"),
        P(),
        P(None, "tp"),
        P("ctx", "tp"),
        P("tp"),
        P("tp"),
        P(),
        P("tp", None),
    )
    return jax.shard_map(per_device, mesh=mesh, in_specs=placed, out_specs=P("ctx", "tp"), check_vma=False)
```

```python
import functools

import jax
import jax.numpy as jnp
from jax import lax
from jax.experimental import pallas as pl
from jax.experimental.pallas import tpu as pltpu
from jax.sharding import PartitionSpec as P

STRETCH = 256
STEPS = 4
HEAD = 64
STATE = 128
LEVELS = 8
BLOCK = 256
GATE_BLOCK = 512
LOG2_E = 1.4426950408889634
F32 = jnp.float32
BF16 = jnp.bfloat16
NT = (((1,), (1,)), ((), ()))
CHUNKS = ((0, 2), (2, 3), (3, 4))
SMEM = pl.BlockSpec(memory_space=pltpu.SMEM)
VMEM = pl.BlockSpec(memory_space=pltpu.VMEM)
FAR = pl.BlockSpec(memory_space=pltpu.HBM)


def dot(a, b):
    return jnp.dot(a, b, preferred_element_type=F32)


def dot_nt(a, b):
    return lax.dot_general(a, b, NT, preferred_element_type=F32)


def iota(shape, dim):
    return lax.broadcasted_iota(jnp.int32, shape, dim)


def far(x):
    return pltpu.with_memory_space_constraint(x, pltpu.HBM)


def twice(x):
    return jnp.concatenate([x, x], axis=1)


def split(x):
    high = x.astype(BF16)
    rest = x - high.astype(F32)
    middle = rest.astype(BF16)
    low = (rest - middle.astype(F32)).astype(BF16)
    return jnp.concatenate([high, middle, low], axis=0)


def running_sums(decays):
    rows = decays.shape[0]
    shape = (STRETCH, STRETCH)
    parts = dot(split(decays), (iota(shape, 0) <= iota(shape, 1)).astype(BF16))
    return (parts[:rows] + parts[rows : 2 * rows]) + parts[2 * rows :]


def lanes(column):
    return jnp.broadcast_to(column, (column.shape[0], STATE))


def store_total(ref, top, total):
    heads = total.shape[0]
    high = total.astype(BF16)
    rest = total - high.astype(F32)
    middle = rest.astype(BF16)
    low = (rest - middle.astype(F32)).astype(BF16)
    ref[pl.ds(top, heads), :] = high
    ref[pl.ds(top + heads, heads), :] = middle
    ref[pl.ds(top + 2 * heads, heads), :] = low


def load_total(ref, top, heads):
    parts = [ref[pl.ds(top + k * heads, heads), :].astype(F32) for k in range(3)]
    return (parts[0] + parts[1]) + parts[2]


def call(kernel, name, in_specs, out_shape, args, scratch=(), mib=8, flops=1 << 20, moved=1 << 20, out_specs=None):
    return pl.pallas_call(
        kernel,
        name=name,
        in_specs=in_specs,
        out_specs=[VMEM] * len(out_shape),
        out_shape=[jax.ShapeDtypeStruct(*x) for x in out_shape],
        scratch_shapes=list(scratch),
        compiler_params=pltpu.CompilerParams(vmem_limit_bytes=mib << 20),
        cost_estimate=pl.CostEstimate(flops=flops, bytes_accessed=moved, transcendentals=0),
    )(*args)


def project_kernel(
    docs, decays_hbm, tok_hbm, value_hbm, state_hbm, tok, sp, v, local, pay, w_value, w_state, tail, grow, scaled, decays,
    sems,
):
    heads = decays.shape[0]
    blocks = w_value.shape[1] // BLOCK
    per_block = BLOCK // HEAD

    def token_copy(i):
        at = pl.ds(i * STRETCH, STRETCH)
        return pltpu.make_async_copy(tok_hbm.at[at, :], tok.at[at, :], sems.at[i])

    def value_copy(k):
        at = pl.ds(k * BLOCK, BLOCK)
        return pltpu.make_async_copy(value_hbm.at[:, at], w_value.at[:, at], sems.at[STEPS + k])

    state_copy = pltpu.make_async_copy(state_hbm, w_state, sems.at[STEPS + blocks])
    decay_copy = pltpu.make_async_copy(decays_hbm, decays, sems.at[STEPS + blocks + 1])
    decay_copy.start()
    token_copy(0).start()
    state_copy.start()
    value_copy(0).start()
    for i in range(1, STEPS):
        token_copy(i).start()
    value_copy(1).start()

    decay_copy.wait()
    stacked = jnp.concatenate([decays[:, pl.ds(i * STRETCH, STRETCH)] for i in range(STEPS)], axis=0)
    cum = running_sums(stacked)
    total = lanes(cum[:, STRETCH - 1 :])
    rest = jnp.exp(twice(total) - cum)
    first = lax.axis_index("ctx") * STEPS
    whole = jnp.zeros((heads, STATE), F32)
    for i in range(STEPS):
        rows = slice(i * heads, (i + 1) * heads)
        tail[:, pl.ds(i * STRETCH, STRETCH)] = rest[rows]
        same = (docs[first + max(i - 1, 0)] == docs[first + i]).astype(F32)
        grow[i] = jnp.exp(total[rows]) * same
        whole = whole + total[rows]
    store_total(pay, heads * HEAD, whole)

    def states(k):
        at = pl.ds(k * BLOCK, BLOCK)
        for h in range(per_block):
            rows = pl.ds(k * BLOCK + h * HEAD, HEAD)
            row = k * per_block + h
            scaled[rows, :] = (v[rows, :].astype(F32) * tail[row : row + 1, :]).astype(BF16)
        run = None
        for i in range(STEPS):
            here = pl.ds(i * STRETCH, STRETCH)
            state = dot(scaled[at, here], sp[here, :STATE])
            if i == 0:
                run = state
                local[0, at, :] = state.astype(BF16)
                continue
            factor = jnp.concatenate(
                [
                    jnp.broadcast_to(grow[i, k * per_block + h : k * per_block + h + 1, :], (HEAD, STATE))
                    for h in range(per_block)
                ],
                axis=0,
            )
            run = run * factor + state
            if i == 1:
                local[1, at, :] = run.astype(BF16)
            if i == 2:
                local[2, at, :] = state.astype(BF16)
        pay[at, :] = run.astype(BF16)

    for k in range(blocks):
        at = pl.ds(k * BLOCK, BLOCK)
        if k:
            value_copy(k).wait()
            for i in range(STEPS):
                here = pl.ds(i * STRETCH, STRETCH)
                v[at, here] = jnp.transpose(dot(tok[here, :], w_value[:, at]).astype(BF16))
            states(k - 1)
        else:
            for i in range(STEPS):
                here = pl.ds(i * STRETCH, STRETCH)
                token_copy(i).wait()
                if i == 0:
                    state_copy.wait()
                sp[here, :] = dot(tok[here, :], w_state[...]).astype(BF16)
                if i == 0:
                    value_copy(0).wait()
                if i == 1:
                    value_copy(2).start()
                if i == 2:
                    value_copy(3).start()
                v[at, here] = jnp.transpose(dot(tok[here, :], w_value[:, at]).astype(BF16))
    states(blocks - 1)


def project(docs, decays, tokens, w_value, w_state):
    rows, depth = tokens.shape
    heads = decays.shape[0]
    width = w_value.shape[1]
    return call(
        project_kernel,
        "project",
        [SMEM, FAR, FAR, FAR, FAR],
        [
            ((rows, depth), BF16),
            ((rows, 2 * STATE), BF16),
            ((width, rows), BF16),
            ((3, width, STATE), BF16),
            ((width + 3 * heads, STATE), BF16),
        ],
        (docs, *(far(x) for x in (decays, tokens, w_value, w_state))),
        [
            pltpu.VMEM((depth, width), BF16),
            pltpu.VMEM((depth, 2 * STATE), BF16),
            pltpu.VMEM((heads, rows), F32),
            pltpu.VMEM((STEPS, heads, STATE), F32),
            pltpu.VMEM((width, rows), BF16),
            pltpu.VMEM((heads, rows), F32),
            pltpu.SemaphoreType.DMA((STEPS + width // BLOCK + 2,)),
        ],
        mib=16,
        flops=2 * rows * depth * (width + 2 * STATE),
        moved=2 * (rows * depth + depth * width),
    )


def joined(docs, last_first, last_second):
    return (docs[last_first] == docs[last_second]).astype(F32)


def half_rows(core, *factors):
    half = factors[0].shape[0] // 2
    return [jnp.where(core == 0, x[:half], x[half:]) for x in factors]


def near_kernel(docs, own, peer, pay, earlier):
    heads = earlier.shape[0]
    half = heads // 2
    ctx = lax.axis_index("ctx")
    core, pair = ctx & 1, ctx >> 1
    second = core == 1
    total_own, total_peer = load_total(own, heads * HEAD, heads), load_total(peer, heads * HEAD, heads)
    keep = joined(docs, pair * 2 * STEPS + STEPS - 1, pair * 2 * STEPS + 2 * STEPS - 1)
    factor = jnp.exp(jnp.where(second, total_own, total_peer)) * keep
    own_by, peer_by = half_rows(core, jnp.where(second, 1.0, factor), jnp.where(second, factor, 1.0))
    for h in range(half):
        at = pl.ds(pl.multiple_of(core * (half * HEAD) + h * HEAD, HEAD), HEAD)
        row = slice(h, h + 1)
        pay[pl.ds(h * HEAD, HEAD), :] = (
            own[at, :].astype(F32) * own_by[row] + peer[at, :].astype(F32) * peer_by[row]
        ).astype(BF16)
    store_total(pay, half * HEAD, total_own + total_peer)
    earlier[...] = jnp.where(second, total_peer, 0.0)


def middle_kernel(docs, own, one, two, three, before, after, pay, left, earlier):
    heads = before.shape[0]
    half = heads // 2
    top = half * HEAD
    ctx = lax.axis_index("ctx")
    core, chip = ctx & 1, ctx >> 1
    odd, high = (chip & 1) == 1, (chip & 2) == 2
    t_own, t_one, t_two, t_three = (load_total(x, top, heads) for x in (own, one, two, three))
    last = lambda at: (at + 1) * 2 * STEPS - 1
    base, mine, theirs = (chip >> 2) << 2, (chip >> 1) << 1, ((chip >> 1) ^ 1) << 1
    keep_mine = joined(docs, last(mine), last(mine + 1))
    keep_theirs = joined(docs, last(theirs), last(theirs + 1))
    keep_all = joined(docs, last(base + 1), last(base + 3))
    by_mine = jnp.exp(jnp.where(odd, t_own, t_one)) * keep_mine
    by_theirs = jnp.exp(jnp.where(odd, t_two, t_three)) * keep_theirs
    by_all = jnp.exp(jnp.where(high, t_own + t_one, t_two + t_three)) * keep_all
    own_by, one_by, two_by, three_by, mine_by, theirs_by = half_rows(
        core,
        jnp.where(odd, 1.0, by_mine),
        jnp.where(odd, by_mine, 1.0),
        jnp.where(odd, 1.0, by_theirs),
        jnp.where(odd, by_theirs, 1.0),
        jnp.where(high, 1.0, by_all),
        jnp.where(high, by_all, 1.0),
    )
    for h in range(half):
        at = pl.ds(h * HEAD, HEAD)
        row = slice(h, h + 1)
        here = own[at, :].astype(F32) * own_by[row] + one[at, :].astype(F32) * one_by[row]
        there = two[at, :].astype(F32) * two_by[row] + three[at, :].astype(F32) * three_by[row]
        left[at, :] = one[at, :]
        left[pl.ds(top + h * HEAD, HEAD), :] = there.astype(BF16)
        pay[at, :] = (here * mine_by[row] + there * theirs_by[row]).astype(BF16)
    store_total(pay, top, (t_own + t_one) + (t_two + t_three))
    second = before[...] + jnp.where(odd, t_one, 0.0)
    earlier[pl.ds(0, heads), :] = second
    earlier[pl.ds(heads, heads), :] = second + jnp.where(high, t_two + t_three, 0.0)


def far_kernel(docs, one, two, three, before, after, left, earlier):
    heads = earlier.shape[0]
    half = heads // 2
    top = half * HEAD
    ctx = lax.axis_index("ctx")
    row_of = ctx >> 3
    odd = (row_of & 1) == 1
    t_one, t_two, t_three = (load_total(x, top, heads) for x in (one, two, three))
    theirs = ((row_of >> 1) ^ 1) << 1
    last = lambda at: (at + 1) * 8 * STEPS - 1
    factor = jnp.exp(jnp.where(odd, t_two, t_three)) * joined(docs, last(theirs), last(theirs + 1))
    two_by, three_by = half_rows(ctx & 1, jnp.where(odd, 1.0, factor), jnp.where(odd, factor, 1.0))
    for h in range(half):
        at = pl.ds(h * HEAD, HEAD)
        row = slice(h, h + 1)
        left[at, :] = one[at, :]
        left[pl.ds(top + h * HEAD, HEAD), :] = (
            two[at, :].astype(F32) * two_by[row] + three[at, :].astype(F32) * three_by[row]
        ).astype(BF16)
    earlier[...] = before[pl.ds(heads, heads), :] + jnp.where(odd, t_one, 0.0)


def assemble(core, own, peer, full):
    half = own.shape[0] // 2
    for level in range(2):
        source = pl.ds(level * half, half)
        full[level, pl.ds(pl.multiple_of(core * half, half), half), :] = own[source, :]
        full[level, pl.ds(pl.multiple_of((1 - core) * half, half), half), :] = peer[source, :]


SEND_ORDER = ((2, 0), (1, 1), (2, 1), (3, 0), (1, 0), (3, 1), (0, 0), (0, 1))


def gate_kernel(tok, w_level, gate_hbm, out_hbm, gates, weight, w_out, w_gate, sems):
    blocks = w_gate.shape[1] // GATE_BLOCK
    tp = lax.axis_index("tp")
    eighth = w_out.shape[1] // len(SEND_ORDER)

    def gate_copy(k):
        at = pl.ds(k * GATE_BLOCK, GATE_BLOCK)
        return pltpu.make_async_copy(gate_hbm.at[:, at], w_gate.at[:, at], sems.at[k])

    def out_copy(j):
        shift, side = SEND_ORDER[j]
        source = pl.ds(pl.multiple_of((((tp + shift) & 3) * 2 + side) * eighth, eighth), eighth)
        return pltpu.make_async_copy(out_hbm.at[:, source], w_out.at[:, pl.ds(j * eighth, eighth)], sems.at[blocks + j])

    for k in range(blocks):
        gate_copy(k).start()
    cols = w_level.shape[1]
    heads = cols // LEVELS
    to_row, from_col = iota((cols, cols), 0), iota((cols, cols), 1)
    pick = ((to_row % heads) * LEVELS + to_row // heads == from_col).astype(BF16)
    turned = dot_nt(pick, dot(tok[...], w_level[...]).astype(BF16))
    weight[...] = jnp.maximum(turned, 0.0) + jnp.log1p(jnp.exp(-jnp.abs(turned)))
    for k in range(blocks):
        gate_copy(k).wait()
        if k == 0:
            for j in range(len(SEND_ORDER)):
                out_copy(j).start()
        at = pl.ds(k * GATE_BLOCK, GATE_BLOCK)
        gates[at, :] = jnp.transpose(dot(tok[...], w_gate[:, at]).astype(BF16))
    for j in range(len(SEND_ORDER)):
        out_copy(j).wait()


def remote_term(docs, ctx, bit, stretch_doc, weight, here, gone, source, c_out):
    heads = weight.shape[0] // LEVELS
    base = (ctx >> (bit + 1)) << (bit + 1)
    last_left = docs[(base + (1 << bit)) * STEPS - 1]
    live = ((((ctx >> bit) & 1) == 1) & (last_left == stretch_doc)).astype(F32)
    rows = weight[pl.ds((bit + 3) * heads, heads), here] * live
    if gone is not None:
        rows = rows * twice(jnp.exp(gone))
    return dot_nt(source[pl.ds(0, heads * HEAD), :], c_out), rows


def intra_kernel(docs, skip, weight, decays, v, sp, local, r0, ho, scaled_weight):
    heads = decays.shape[0]
    ctx = lax.axis_index("ctx")
    first = ctx * STEPS
    causal = iota((128, 128), 0) <= iota((128, 128), 1)
    lower = (iota((STRETCH, STRETCH), 0) >= iota((STRETCH, STRETCH), 1)).astype(BF16)
    begin = jnp.zeros((heads, STATE), F32)
    previous = begin
    for index in range(STEPS):
        here = pl.ds(index * STRETCH, STRETCH)
        now = decays[:, here]
        cum = running_sums(now)
        parts = dot_nt(lower, split(now))
        cum_col = (parts[:, :heads] + parts[:, heads : 2 * heads]) + parts[:, 2 * heads :]
        total = lanes(cum[:, STRETCH - 1 :])
        grown = jnp.exp(cum)
        from_device = jnp.exp(cum + twice(begin))
        for level in range(3, LEVELS):
            rows = pl.ds(level * heads, heads)
            scaled_weight[rows, here] = weight[rows, here] * from_device
        b_in, c_out = sp[here, :STATE], sp[here, STATE:]
        scores = dot_nt(b_in, c_out)
        terms = []
        if index & 1:
            keep = joined(docs, first + index - 1, first + index)
            terms.append((0 if index == 1 else 2, weight[pl.ds(heads, heads), here] * grown * keep))
        if index & 2:
            keep = joined(docs, first + 1, first + index)
            factor = grown * jnp.exp(twice(previous)) if index == 3 else grown
            terms.append((1, weight[pl.ds(2 * heads, heads), here] * factor * keep))
        crosses = [(dot_nt(local[slot], c_out), row) for slot, row in terms]
        stretch_doc = docs[first + index]
        crosses.append(remote_term(docs, ctx, 0, stretch_doc, scaled_weight, here, None, r0, c_out))
        own_weight = weight[pl.ds(0, heads), here]
        cum2, cum_col2 = cum * LOG2_E, cum_col * LOG2_E
        for h in range(heads):
            at = slice(h * HEAD, (h + 1) * HEAD)
            col = cum_col2[:, h : h + 1]
            row = cum2[h : h + 1, :]

            def block(s, t, masked):
                decay = jnp.exp2(
                    jnp.broadcast_to(row[:, t * 128 : t * 128 + 128], (128, 128)) - col[s * 128 : s * 128 + 128, :]
                )
                if masked:
                    decay = jnp.where(causal, decay, 0.0)
                return (scores[s * 128 : s * 128 + 128, t * 128 : t * 128 + 128] * decay).astype(BF16)

            vh = v[pl.ds(h * HEAD, HEAD), here]
            left = dot(vh[:, :128], block(0, 0, True))
            right = dot(vh, jnp.concatenate([block(0, 1, False), block(1, 1, True)], axis=0))
            out = skip[h] * vh.astype(F32) + own_weight[h : h + 1, :] * jnp.concatenate([left, right], axis=1)
            for cross, factor in crosses:
                out = out + factor[h : h + 1, :] * cross[at]
            ho[pl.ds(h * HEAD, HEAD), here] = out
        begin = begin + total
        previous = total


def late_kernel(docs, sp, ho, weight, e1, e23, own, peer, out, full):
    heads = e1.shape[0]
    ctx = lax.axis_index("ctx")
    assemble(ctx & 1, own, peer, full)
    for index in range(STEPS):
        here = pl.ds(index * STRETCH, STRETCH)
        c_out = sp[here, STATE:]
        stretch_doc = docs[ctx * STEPS + index]
        terms = [
            remote_term(docs, ctx, bit, stretch_doc, weight, here, gone, full.at[bit - 1], c_out)
            for bit, gone in ((1, e1[...]), (2, e23[pl.ds(0, heads), :]))
        ]
        for h in range(heads):
            at = pl.ds(h * HEAD, HEAD)
            total = ho[at, here]
            for cross, rows in terms:
                total = total + rows[h : h + 1, :] * cross[h * HEAD : (h + 1) * HEAD]
            out[at, here] = total


def finish_kernel(
    start, count, docs, gain, w_out, sp, gates, ho, weight, e23, e4, *refs
):
    far_own, far_peer, plus, minus, normed, acc, full = refs
    ctx = lax.axis_index("ctx")
    heads = e4.shape[0]
    assemble(ctx & 1, far_own, far_peer, full)
    for j in range(count):
        here = pl.ds((start + j) * STRETCH, STRETCH)
        c_out = sp[here, STATE:]
        stretch_doc = docs[ctx * STEPS + start + j]
        terms = [
            remote_term(docs, ctx, bit, stretch_doc, weight, here, gone, full.at[bit - 3], c_out)
            for bit, gone in ((3, e23[pl.ds(heads, heads), :]), (4, e4[...]))
        ]
        for h in range(heads):
            at = pl.ds(h * HEAD, HEAD)
            total = ho[at, here]
            for cross, rows in terms:
                total = total + rows[h : h + 1, :] * cross[h * HEAD : (h + 1) * HEAD]
            g = gates[at, here].astype(F32)
            gated = total * (g / (1.0 + jnp.exp(-g)))
            power = jnp.sum(gated * gated, axis=0, keepdims=True) * (1.0 / HEAD)
            acc[at, :] = gated * lax.rsqrt(power + 1e-5)
        normed[pl.ds(j * STRETCH, STRETCH), :] = (jnp.transpose(acc[...]) * gain[...]).astype(BF16)
    quarter = w_out.shape[1] // 4
    for j, out in enumerate((plus, minus)):
        out[...] = dot(normed[...], w_out[:, pl.ds(j * quarter, quarter)]).astype(BF16)


def stay_kernel(normed, w_out, keep, own):
    quarter = w_out.shape[1] // 4
    for j, out in enumerate((keep, own)):
        out[...] = dot(normed[...], w_out[:, pl.ds((j + 2) * quarter, quarter)]).astype(BF16)


def stay(start, normed, w_out):
    rows, width = normed.shape
    depth = w_out.shape[1]
    return call(
        stay_kernel,
        f"stay{start}",
        [VMEM] * 2,
        [((rows, depth // 4), BF16)] * 2,
        (normed, w_out),
        mib=8,
        flops=rows * depth * width,
        moved=1 << 20,
    )


def finish(start, stop, docs, gain, w_out, *operands):
    count = stop - start
    width, depth = w_out.shape
    rows = count * STRETCH
    return call(
        functools.partial(finish_kernel, start, count),
        f"finish{start}",
        [SMEM] + [VMEM] * (2 + len(operands)),
        [((rows, depth // 4), BF16)] * 2 + [((rows, width), BF16)],
        (docs, gain, w_out, *operands),
        [
            pltpu.VMEM((width, STRETCH), F32),
            pltpu.VMEM((2, width, STATE), BF16),
        ],
        mib=16,
        flops=2 * rows * depth * width,
        moved=2 * width * depth + 8 * rows * width,
    )


def per_device(tokens, w_value, w_gate, w_state, w_level, log_decay, skip_weight, norm_gain, doc_ids, w_out):
    rows, depth = tokens.shape
    width = w_value.shape[1]
    heads = log_decay.shape[1]
    docs = far(doc_ids)
    decays = jnp.transpose(log_decay)
    part = ((width // 2 + 3 * heads, STATE), BF16)
    tail = ((width, STATE), BF16)
    gone = ((heads, STATE), F32)

    def across(x, by):
        return lax.ppermute(x, "ctx", [(i, i ^ by) for i in range(32)])

    def turn(x, by):
        return lax.ppermute(x, "tp", [(i, (i + by) % 4) for i in range(4)])

    tok, sp, v, local, pay0 = project(docs, decays, tokens, w_value, w_state)
    peer = across(pay0, 1)
    pay1, e1 = call(
        near_kernel, "near", [SMEM] + [VMEM] * 2, [part, gone], (docs, pay0, peer)
    )
    ys = [across(pay1, by) for by in (4, 2, 6)]
    gates, weight, w_out_near = call(
        gate_kernel,
        "gate",
        [VMEM] * 2 + [FAR] * 2,
        [((width, rows), BF16), ((heads * LEVELS, rows), F32), (w_out.shape, BF16)],
        (tok, w_level, far(w_gate), far(w_out)),
        [pltpu.VMEM(w_gate.shape, BF16), pltpu.SemaphoreType.DMA((width // GATE_BLOCK + len(SEND_ORDER),))],
        mib=16,
        flops=2 * rows * depth * (width + STATE),
        moved=2 * (rows * depth + depth * width),
    )
    y2, y1, y3 = ys
    pay2, mid_own, e23 = call(
        middle_kernel,
        "middle",
        [SMEM] + [VMEM] * 6,
        [part, tail, ((2 * heads, STATE), F32)],
        (docs, pay1, y1, y2, y3, e1, weight),
    )
    x2, x1, x3 = (across(pay2, by) for by in (16, 8, 24))
    mid_peer = across(mid_own, 1)
    ho, scaled_weight = call(
        intra_kernel,
        "intra",
        [SMEM] * 2 + [VMEM] * 6,
        [((width, rows), F32), ((heads * LEVELS, rows), F32)],
        (docs, skip_weight, weight, decays, v, sp, local, peer),
        mib=12,
        flops=6 << 30,
        moved=8 << 20,
    )
    far_own, e4 = call(
        far_kernel,
        "far",
        [SMEM] + [VMEM] * 5,
        [tail, gone],
        (docs, x1, x2, x3, e23, scaled_weight),
    )
    far_peer = across(far_own, 1)
    (ho,) = call(
        late_kernel,
        "late",
        [SMEM] + [VMEM] * 7,
        [((width, rows), F32)],
        (docs, sp, ho, scaled_weight, e1, e23, mid_own, mid_peer),
        [pltpu.VMEM((2, width, STATE), BF16)],
        mib=8,
        flops=2 << 30,
        moved=4 << 20,
    )
    gain = norm_gain.reshape(1, -1)
    results = []
    half = w_out.shape[1] // 8
    for lo, hi in CHUNKS:
        plus, minus, normed = finish(
            lo, hi, docs, gain, w_out_near, sp, gates, ho, scaled_weight, e23, e4, far_own, far_peer
        )
        from_below, from_above = turn(plus, 1), turn(minus, 3)
        keep, own = stay(lo, normed, w_out_near)
        on_plus = (keep[:, :half].astype(F32) + from_below[:, :half].astype(F32)).astype(BF16)
        on_minus = (keep[:, half:].astype(F32) + from_above[:, :half].astype(F32)).astype(BF16)
        last_below, last_above = turn(on_plus, 1), turn(on_minus, 3)
        first = own[:, :half].astype(F32) + from_above[:, half:].astype(F32) + last_below.astype(F32)
        second = own[:, half:].astype(F32) + from_below[:, half:].astype(F32) + last_above.astype(F32)
        results.append(jnp.concatenate([first, second], axis=1).astype(BF16))
    return jnp.concatenate(results, axis=0)


def solution(mesh):
    placed = (
        P("ctx", None),
        P(None, "tp"),
        P(None, "tp"),
        P(),
        P(None, "tp"),
        P("ctx", "tp"),
        P("tp"),
        P("tp"),
        P(),
        P("tp", None),
    )
    return jax.shard_map(per_device, mesh=mesh, in_specs=placed, out_specs=P("ctx", "tp"), check_vma=False)
```
